32 devices in a mesh: fsdp: 32 (over z, y, x, core).
Axes of the slice: x: 2, y: 2, z: 4, core: 2. Of those that a mesh axis runs over, the one named last changes fastest.
Arguments:
- tokens: bfloat16 [4096, 768], P('fsdp'), may hold values from -6 to 6
- seq_lengths: int32 [32, 8], P('fsdp'), may hold values from 1 to 64, 128 in all within a row
- cotangent: bfloat16 [4096, 768], P('fsdp'), may hold values from -6 to 6
- wide_weights: float32 [768, 6144], P('fsdp'), may hold values from -2 to 2
- proj_weights: float32 [3072, 768], P('fsdp'), may hold values from -0.109375 to 0.109375
- vector_params: float32 [12, 768], P(None, 'fsdp'), may hold values from -1 to 1.5
- wide_moments: float32 [2, 768, 6144], P(None, 'fsdp'), may hold values from -0.16 to 0.16, as said below
- proj_moments: float32 [2, 3072, 768], P(None, 'fsdp'), may hold values from -0.16 to 0.16, as said below
- vector_moments: float32 [2, 12, 768], P(None, None, 'fsdp'), may hold values from -0.16 to 0.16, as said below
Outputs:
- block_output: bfloat16 [4096, 768], P('fsdp')
- tokens_grad: bfloat16 [4096, 768], P('fsdp')
- wide_grad: float32 [768, 6144], P('fsdp')
- proj_grad: float32 [3072, 768], P('fsdp')
- vector_grad: float32 [12, 768], P(None, 'fsdp')
- wide_new: float32 [768, 6144], P('fsdp')
- proj_new: float32 [3072, 768], P('fsdp')
- vector_new: float32 [12, 768], P(None, 'fsdp')
- wide_moments_new: float32 [2, 768, 6144], P(None, 'fsdp')
- proj_moments_new: float32 [2, 3072, 768], P(None, 'fsdp')
- vector_moments_new: float32 [2, 12, 768], P(None, None, 'fsdp')
The draws below stay inside these ranges and needn't reach their ends.
Inputs may be any that keep to these rules, and one draw needn't show every extreme that they name: `seq_lengths`: row s holds the lengths of the 8 sequences of device slice s; every row sums to 128 and its largest entry is 64. `wide_moments`: index 0 of the leading dimension holds first moments, index 1 second moments, which are positive. `proj_moments`: index 0 of the leading dimension holds first moments, index 1 second moments, which are positive. `vector_moments`: index 0 of the leading dimension holds first moments, index 1 second moments, which are positive.
All inputs are finite; a program needn't handle non-finite values.
Results may differ from the reference program's by a relative error of at most 0.012.
The reference program's roundings to bfloat16 on the way count: a program that leaves them out, or rounds other values in their place, can miss the bound.
Values may be sent and summed in bfloat16 or wider, within the bound.
A program may use at most 192 MiB of HBM per device.

```python
import math
import jax
import jax.numpy as jnp
import numpy as np
from jax import lax

D = 768
H = 12
HD = 64
FF = 3072
TOK_DEV = 128
SEQS_DEV = 8
STEP = 2
LMAX = 64
TOKENS = 4096
SLICES = 32
VROWS = 12
N_FSDP = 32


def draw_wide_weights(key, part):
    base_key = jax.random.fold_in(key, 0)
    standard = jax.random.normal(base_key, (D, 4 * D + FF), jnp.float32) / math.sqrt(D)
    column = jnp.arange(4 * D + FF)
    factor = jnp.where((column >= 3 * D) & (column < 4 * D), 4.0, 1.0)
    sampled = standard * factor[None, :]
    return jnp.clip(sampled, -2.0, 2.0)


def draw_vector_params(key, part):
    gain_key, shift_key = jax.random.split(key)
    row_index = jnp.arange(VROWS)[:, None]
    gains = jax.random.uniform(gain_key, (VROWS, D), jnp.float32, 0.5, 1.5)
    shifts = jnp.clip(0.3 * jax.random.normal(shift_key, (VROWS, D), jnp.float32), -1.0, 1.0)
    is_gain = (row_index == 0) | (row_index == 5)
    return jnp.where(is_gain, gains, shifts)


def draw_moment_pair(key, shape):
    first_key, second_key = jax.random.split(key)
    signed = jnp.clip(jax.random.normal(first_key, shape, jnp.float32), -4.0, 4.0) * 0.04
    log_low = math.log(0.0005)
    log_high = math.log(0.01)
    positive = jnp.exp(jax.random.uniform(second_key, shape, jnp.float32, log_low, log_high))
    return jnp.stack([signed, positive])


def draw_wide_moments(key, part):
    return draw_moment_pair(key, (D, 4 * D + FF))


def draw_proj_moments(key, part):
    return draw_moment_pair(key, (FF, D))


def draw_vector_moments(key, part):
    return draw_moment_pair(key, (VROWS, D))


def raised(array, rng, source, target, blocks, factor):
    owner, partner = [(jnp.arange(array.shape[dim]) // (array.shape[dim] // blocks)).reshape([-1 if axis == dim else 1 for axis in range(array.ndim)]) for dim in (source, target)]
    chosen = jax.random.permutation(rng, blocks)[partner]
    strong = (owner == chosen) | (owner == (partner + blocks // 2) % blocks)
    return jnp.where(strong, factor * array, array)


def block_levels(stream_key, shape, shards, least, top_value):
    def one(dim, blocks):
        draws = jax.random.uniform(jax.random.fold_in(jax.random.fold_in(stream_key, 6), dim), (blocks,), jnp.float32, least / len(shards), top_value / len(shards))
        return jnp.repeat(jnp.exp(draws), shape[dim] // blocks).reshape((-1,) + (1,) * (len(shape) - dim - 1))

    factor_of = one(*shards[0])
    for cut in shards[1:]:
        factor_of = factor_of * one(*cut)
    return factor_of


def length_profile(number_of, total, bound, slope):
    loads = [(1 << 20) // math.isqrt(grade ** slope) + 1 for grade in range(2, number_of + 1)]
    spare, counts = total - bound - (number_of - 1), [1] * (number_of - 1)
    while spare > 0:
        candidates = [i for i in range(number_of - 1) if counts[i] < bound]
        mass, remaining = sum([loads[i] for i in candidates]), spare
        for i in candidates:
            addition = min(bound - counts[i], max(1, remaining * loads[i] // mass), spare)
            counts[i] = counts[i] + addition
            spare = spare - addition
    return np.array([bound] + counts)


def uneven_parts(rng, number_of, total, bound, slope):
    if number_of == 2:
        one = jax.random.randint(rng, (), max(1, total - bound), min(bound, total - 1) + 1)
        return jnp.stack([one, total - one])
    sizes = jnp.asarray(length_profile(number_of, total, bound, slope), jnp.int32)
    couples = (number_of - 1) // 2
    giver, taker = sizes[1:1 + 2 * couples:2], sizes[2:2 + 2 * couples:2]
    room = jnp.minimum(giver - 1, bound - taker)
    shifted = jax.random.randint(jax.random.fold_in(rng, 1), (couples,), 0, 1 << 20) % (room + 1)
    sizes = sizes.at[1:1 + 2 * couples:2].set(giver - shifted).at[2:2 + 2 * couples:2].set(taker + shifted)
    return sizes[jax.random.permutation(jax.random.fold_in(rng, 2), number_of)]


def bell_draw(key, extent, spread, reach, cuts=(), kind=jnp.bfloat16):
    loudness = block_levels(key, extent, cuts, -0.22, 0.18) if cuts else 1.0
    entries = jax.random.normal(key, extent, jnp.float32) * spread * loudness
    return jnp.minimum(jnp.maximum(entries, -reach), reach).astype(kind)


def heavy_noise(stream_key, dims, width, most, cuts, heavy, held_as=jnp.bfloat16):
    array = width * jax.random.normal(stream_key, dims, jnp.float32)
    if cuts:
        array = array * block_levels(stream_key, dims, cuts, -0.22, 0.18)
    return jnp.clip(raised(array, jax.random.fold_in(stream_key, 3), *heavy), -most, most).astype(held_as)


def setup_inputs(seed: int = 0) -> dict:
    key_of = jax.random.split(jax.random.key(seed), 10)
    return {
        "tokens": bell_draw(key_of[0], (TOKENS, D), 1.0, 6.0, ((0, 32),)),
        "seq_lengths": jax.vmap(lambda own: uneven_parts(own, SEQS_DEV, TOK_DEV, LMAX, 2))(jax.random.split(key_of[1], SLICES)).reshape((SLICES, SEQS_DEV)).astype(jnp.int32),
        "cotangent": heavy_noise(key_of[2], (TOKENS, D), 1.0, 6.0, ((0, 32),), (0, 1, 32, 2.75)),
        "wide_weights": draw_wide_weights(jax.random.fold_in(key_of[9], 71), 0),
        "proj_weights": bell_draw(key_of[4], (FF, D), FF ** -0.5, 0.109375, ((0, 32),), jnp.float32),
        "vector_params": draw_vector_params(jax.random.fold_in(key_of[9], 71), 0),
        "wide_moments": draw_wide_moments(jax.random.fold_in(key_of[9], 71), 0),
        "proj_moments": draw_proj_moments(jax.random.fold_in(key_of[9], 71), 0),
        "vector_moments": draw_vector_moments(jax.random.fold_in(key_of[9], 71), 0),
    }


norm_eps = 1e-05
beta_one = 0.9
beta_two = 0.95
adam_eps = 1e-08
rate_matrix = 0.02
rate_vector = 0.2
weight_decay = 0.1
gelu_coeff = 0.7978845608028654
masked_score = -1e+30

def to_half(values):
    return lax.optimization_barrier(values.astype(jnp.bfloat16))

def norm_forward(values, gain_row, offset):
    center = values - lax.optimization_barrier(jnp.mean(values, axis=1, keepdims=True))
    variance = lax.optimization_barrier(jnp.mean(center * center, axis=1, keepdims=True))
    inverse = lax.rsqrt(variance + norm_eps)
    normed = center * inverse
    return (normed * gain_row + offset, normed, inverse)

def norm_backward(upstream, normed, inverse, gain_row):
    scaled = upstream * gain_row
    mean_term = lax.optimization_barrier(jnp.mean(scaled, axis=1, keepdims=True))
    proj_term = lax.optimization_barrier(jnp.mean(scaled * normed, axis=1, keepdims=True))
    input_grad = inverse * (scaled - mean_term - normed * proj_term)
    return (input_grad, lax.optimization_barrier(jnp.sum(upstream * normed, axis=0)), lax.optimization_barrier(jnp.sum(upstream, axis=0)))

def gelu_parts(before):
    inner_arg = gelu_coeff * (before + 0.044715 * before * before * before)
    tangent = jnp.tanh(inner_arg)
    value_part = 0.5 * before * (1.0 + tangent)
    slope_part = 0.5 * (1.0 + tangent) + 0.5 * before * (1.0 - tangent * tangent) * gelu_coeff * (1.0 + 3.0 * 0.044715 * before * before)
    return (value_part, slope_part)

def allowed_pairs(length_row, row_count):
    bounds = jnp.cumsum(length_row.astype(jnp.int32))
    position = jnp.arange(row_count, dtype=jnp.int32)
    segment = lax.optimization_barrier(jnp.sum((position[:, None] >= bounds[None, :]).astype(jnp.int32), axis=1))
    return (segment[:, None] == segment[None, :]) & (position[None, :] <= position[:, None])

def head_view(matrix):
    return matrix.astype(jnp.float32).reshape(matrix.shape[0], H, HD)

def score_table(queries, key_rows, allowed):
    scale_factor = 1.0 / math.sqrt(HD)
    scores = jnp.einsum('qhd,khd->hqk', head_view(queries), head_view(key_rows)) * scale_factor
    return jnp.where(allowed[None, :, :], scores, masked_score)

def attention_forward(queries, key_rows, value_rows, allowed):
    scores = score_table(queries, key_rows, allowed)
    highest = lax.optimization_barrier(jnp.max(scores, axis=2, keepdims=True))
    logsum = highest + jnp.log(lax.optimization_barrier(jnp.sum(jnp.exp(scores - highest), axis=2, keepdims=True)))
    weights = to_half(jnp.exp(scores - logsum)).astype(jnp.float32)
    mixed = jnp.einsum('hqk,khd->qhd', weights, head_view(value_rows))
    return (to_half(mixed.reshape(queries.shape[0], D)), logsum)

def attention_backward(queries, key_rows, value_rows, allowed, logsum, upstream):
    scale_factor = 1.0 / math.sqrt(HD)
    scores = score_table(queries, key_rows, allowed)
    probs = jnp.exp(scores - logsum)
    rounded = to_half(probs).astype(jnp.float32)
    grad_heads = head_view(upstream)
    value_grad = jnp.einsum('hqk,qhd->khd', rounded, grad_heads)
    prob_grad = jnp.einsum('qhd,khd->hqk', grad_heads, head_view(value_rows))
    delta_row = lax.optimization_barrier(jnp.sum(probs * prob_grad, axis=2, keepdims=True))
    score_grad = to_half(probs * (prob_grad - delta_row) * scale_factor).astype(jnp.float32)
    query_grad = jnp.einsum('hqk,khd->qhd', score_grad, head_view(key_rows))
    key_grad = jnp.einsum('hqk,qhd->khd', score_grad, head_view(queries))
    row_total = queries.shape[0]
    joined = jnp.concatenate([query_grad.reshape(row_total, D), key_grad.reshape(row_total, D), value_grad.reshape(row_total, D)], axis=1)
    return to_half(joined)

def slice_pass(token_rows, cot_rows, length_row, wide_half, proj_half, vector_half):
    vectors = vector_half.astype(jnp.float32)
    gain_one, shift_one, query_bias, value_bias = (vectors[0], vectors[1], vectors[2], vectors[3])
    out_bias, gain_two, shift_two, proj_bias = (vectors[4], vectors[5], vectors[6], vectors[7])
    fc_bias = vectors[8:].reshape(FF)
    qkv_weights = wide_half[:, :3 * D]
    out_weights = wide_half[:, 3 * D:4 * D]
    fc_weights = wide_half[:, 4 * D:]
    row_count = token_rows.shape[0]
    allowed = allowed_pairs(length_row, row_count)
    token_float = token_rows.astype(jnp.float32)
    first_norm, normed_one, inverse_one = norm_forward(token_float, gain_one, shift_one)
    first_in = to_half(first_norm)
    qkv_bias = jnp.concatenate([query_bias, jnp.zeros_like(query_bias), value_bias])
    qkv_half = to_half(jnp.dot(first_in, qkv_weights, preferred_element_type=jnp.float32) + qkv_bias)
    queries = qkv_half[:, :D]
    key_rows = qkv_half[:, D:2 * D]
    value_rows = qkv_half[:, 2 * D:]
    attended, logsum = attention_forward(queries, key_rows, value_rows, allowed)
    residual = token_float + jnp.dot(attended, out_weights, preferred_element_type=jnp.float32) + out_bias
    second_norm, normed_two, inverse_two = norm_forward(residual, gain_two, shift_two)
    second_in = to_half(second_norm)
    before_act = jnp.dot(second_in, fc_weights, preferred_element_type=jnp.float32) + fc_bias
    value_part, slope_part = gelu_parts(before_act)
    hidden = to_half(value_part)
    block_rows = (residual + jnp.dot(hidden, proj_half, preferred_element_type=jnp.float32) + proj_bias).astype(jnp.bfloat16)
    cot_float = cot_rows.astype(jnp.float32)
    proj_bias_grad = lax.optimization_barrier(jnp.sum(cot_float, axis=0))
    proj_grad = jnp.dot(hidden.T, cot_rows, preferred_element_type=jnp.float32)
    hidden_grad = jnp.dot(cot_rows, proj_half.T, preferred_element_type=jnp.float32)
    pre_grad = to_half(hidden_grad * slope_part)
    fc_bias_grad = lax.optimization_barrier(jnp.sum(pre_grad.astype(jnp.float32), axis=0))
    fc_grad = jnp.dot(second_in.T, pre_grad, preferred_element_type=jnp.float32)
    second_grad = jnp.dot(pre_grad, fc_weights.T, preferred_element_type=jnp.float32)
    resid_norm_grad, gain_two_grad, shift_two_grad = norm_backward(second_grad, normed_two, inverse_two, gain_two)
    resid_grad = cot_float + resid_norm_grad
    resid_half = to_half(resid_grad)
    out_bias_grad = lax.optimization_barrier(jnp.sum(resid_grad, axis=0))
    out_grad = jnp.dot(attended.T, resid_half, preferred_element_type=jnp.float32)
    attended_grad = to_half(jnp.dot(resid_half, out_weights.T, preferred_element_type=jnp.float32))
    qkv_grad = attention_backward(queries, key_rows, value_rows, allowed, logsum, attended_grad)
    query_bias_grad = lax.optimization_barrier(jnp.sum(qkv_grad[:, :D].astype(jnp.float32), axis=0))
    value_bias_grad = lax.optimization_barrier(jnp.sum(qkv_grad[:, 2 * D:].astype(jnp.float32), axis=0))
    qkv_weight_grad = jnp.dot(first_in.T, qkv_grad, preferred_element_type=jnp.float32)
    first_grad = jnp.dot(qkv_grad, qkv_weights.T, preferred_element_type=jnp.float32)
    token_norm_grad, gain_one_grad, shift_one_grad = norm_backward(first_grad, normed_one, inverse_one, gain_one)
    token_grad_rows = (resid_grad + token_norm_grad).astype(jnp.bfloat16)
    wide_part = jnp.concatenate([qkv_weight_grad, out_grad, fc_grad], axis=1)
    vector_part = jnp.concatenate([jnp.stack([gain_one_grad, shift_one_grad, query_bias_grad, value_bias_grad, out_bias_grad, gain_two_grad, shift_two_grad, proj_bias_grad]), fc_bias_grad.reshape(FF // D, D)], axis=0)
    return (block_rows, token_grad_rows, wide_part, proj_grad, vector_part)

def adam_update(weights, moments, gradient, rate, decay_rate, unscale):
    scaled_grad = gradient / unscale
    first_moment = beta_one * moments[0] + (1.0 - beta_one) * scaled_grad
    second_moment = beta_two * moments[1] + (1.0 - beta_two) * scaled_grad * scaled_grad
    corrected_first = first_moment / (1.0 - beta_one ** STEP)
    corrected_second = second_moment / (1.0 - beta_two ** STEP)
    updated = weights - rate * (corrected_first / (jnp.sqrt(corrected_second) + adam_eps) + decay_rate * weights)
    return (updated, jnp.stack([first_moment, second_moment]))

def reference(tokens, seq_lengths, cotangent, wide_weights, proj_weights, vector_params, wide_moments, proj_moments, vector_moments):
    wide_half = to_half(wide_weights)
    proj_half = to_half(proj_weights)
    vector_half = to_half(vector_params)

    def one_slice(carry, inputs):
        token_rows, cot_rows, length_row = inputs
        block_rows, token_grad_rows, wide_part, proj_part, vector_part = slice_pass(token_rows, cot_rows, length_row, wide_half, proj_half, vector_half)
        carry_next = (carry[0] + wide_part, carry[1] + proj_part, carry[2] + vector_part)
        return (carry_next, (block_rows, token_grad_rows))
    start_sums = (jnp.zeros((D, 4 * D + FF), jnp.float32), jnp.zeros((FF, D), jnp.float32), jnp.zeros((8 + FF // D, D), jnp.float32))
    sliced = (tokens.reshape(N_FSDP, TOK_DEV, D), cotangent.reshape(N_FSDP, TOK_DEV, D), seq_lengths)
    sums, (block_all, grad_all) = lax.scan(one_slice, start_sums, sliced)
    wide_grad, proj_grad, vector_grad = sums
    unscale = math.sqrt(N_FSDP * TOK_DEV)
    wide_new, wide_moments_new = adam_update(wide_weights, wide_moments, wide_grad, rate_matrix, weight_decay, unscale)
    proj_new, proj_moments_new = adam_update(proj_weights, proj_moments, proj_grad, rate_matrix, weight_decay, unscale)
    vector_new, vector_moments_new = adam_update(vector_params, vector_moments, vector_grad, rate_vector, 0.0, unscale)
    block_output = block_all.reshape(N_FSDP * TOK_DEV, D)
    tokens_grad = grad_all.reshape(N_FSDP * TOK_DEV, D)
    return (block_output, tokens_grad, wide_grad, proj_grad, vector_grad, wide_new, proj_new, vector_new, wide_moments_new, proj_moments_new, vector_moments_new)
```

```python
import functools
import math

import jax
import jax.numpy as jnp
from jax import lax
from jax.experimental import pallas as pl
from jax.experimental.pallas import tpu as pltpu
from jax.sharding import PartitionSpec as P

D = 768
H = 12
HD = 64
FF = 3072
STEP = 2


norm_eps = 1e-05
beta_one = 0.9
beta_two = 0.95
adam_eps = 1e-08
rate_matrix = 0.02
rate_vector = 0.2
weight_decay = 0.1
gelu_coeff = 0.7978845608028654
masked_score = -1e30


def norm_forward(values, gain_row, offset):
    center = values - jnp.mean(values, axis=1, keepdims=True)
    variance = jnp.mean(center * center, axis=1, keepdims=True)
    inverse = lax.rsqrt(variance + norm_eps)
    normed = center * inverse
    return (normed * gain_row + offset, normed, inverse)


def norm_backward(upstream, normed, inverse, gain_row):
    scaled = upstream * gain_row
    mean_term = jnp.mean(scaled, axis=1, keepdims=True)
    proj_term = jnp.mean(scaled * normed, axis=1, keepdims=True)
    input_grad = inverse * (scaled - mean_term - normed * proj_term)
    return (input_grad, jnp.sum(upstream * normed, axis=0), jnp.sum(upstream, axis=0))


def gelu_parts(before):
    inner_arg = gelu_coeff * (before + 0.044715 * before * before * before)
    tangent = jnp.tanh(inner_arg)
    value_part = 0.5 * before * (1.0 + tangent)
    slope_part = 0.5 * (1.0 + tangent) + 0.5 * before * (1.0 - tangent * tangent) * gelu_coeff * (
        1.0 + 3.0 * 0.044715 * before * before
    )
    return (value_part, slope_part)


def allowed_pairs(length_row, row_count):
    order = jnp.arange(length_row.shape[0], dtype=jnp.int32)
    bounds = jnp.sum(jnp.where(order[None, :] <= order[:, None], length_row[None, :], 0), axis=1)
    position = jnp.arange(row_count, dtype=jnp.int32)
    segment = jnp.sum((position[:, None] >= bounds[None, :]).astype(jnp.int32), axis=1)
    return (segment[:, None] == segment[None, :]) & (position[None, :] <= position[:, None])


def head_view(matrix):
    return matrix.reshape(matrix.shape[0], H, HD)


def score_table(queries, key_rows, allowed):
    scale_factor = 1.0 / math.sqrt(HD)
    scores = (
        jnp.einsum(
            "qhd,khd->hqk",
            head_view(queries),
            head_view(key_rows),
            preferred_element_type=jnp.float32,
        )
        * scale_factor
    )
    return jnp.where(allowed[None, :, :], scores, masked_score)


def attention_forward(queries, key_rows, value_rows, allowed):
    scores = score_table(queries, key_rows, allowed)
    highest = jnp.max(scores, axis=2, keepdims=True)
    logsum = highest + jnp.log(jnp.sum(jnp.exp(scores - highest), axis=2, keepdims=True))
    weights = jnp.exp(scores - logsum).astype(jnp.bfloat16)
    mixed = jnp.einsum(
        "hqk,khd->qhd", weights, head_view(value_rows), preferred_element_type=jnp.float32
    )
    return (mixed.reshape(queries.shape[0], D).astype(jnp.bfloat16), logsum)


def attention_backward(queries, key_rows, value_rows, allowed, logsum, upstream):
    scale_factor = 1.0 / math.sqrt(HD)
    scores = score_table(queries, key_rows, allowed)
    probs = jnp.exp(scores - logsum)
    rounded = probs.astype(jnp.bfloat16)
    grad_heads = head_view(upstream)
    value_grad = jnp.einsum("hqk,qhd->khd", rounded, grad_heads, preferred_element_type=jnp.float32)
    prob_grad = jnp.einsum(
        "qhd,khd->hqk", grad_heads, head_view(value_rows), preferred_element_type=jnp.float32
    )
    delta_row = jnp.sum(probs * prob_grad, axis=2, keepdims=True)
    score_grad = (probs * (prob_grad - delta_row) * scale_factor).astype(jnp.bfloat16)
    query_grad = jnp.einsum(
        "hqk,khd->qhd", score_grad, head_view(key_rows), preferred_element_type=jnp.float32
    )
    key_grad = jnp.einsum(
        "hqk,qhd->khd", score_grad, head_view(queries), preferred_element_type=jnp.float32
    )
    row_total = queries.shape[0]
    joined = jnp.concatenate(
        [
            query_grad.reshape(row_total, D),
            key_grad.reshape(row_total, D),
            value_grad.reshape(row_total, D),
        ],
        axis=1,
    )
    return joined.astype(jnp.bfloat16)


def adam_update(weights, moments, gradient, rate, decay_rate, unscale):
    scaled_grad = gradient / unscale
    first_moment = beta_one * moments[0] + (1.0 - beta_one) * scaled_grad
    second_moment = beta_two * moments[1] + (1.0 - beta_two) * scaled_grad * scaled_grad
    corrected_first = first_moment / (1.0 - beta_one**STEP)
    corrected_second = second_moment / (1.0 - beta_two**STEP)
    updated = weights - rate * (
        corrected_first / (jnp.sqrt(corrected_second) + adam_eps) + decay_rate * weights
    )
    return (updated, jnp.stack([first_moment, second_moment]))


def column_term(left, right):
    return jnp.einsum("tc,te->ce", left, right, preferred_element_type=jnp.float32)


MESH = pl.DeviceIdType.MESH
WIDE_A = 6 * D
GROUP = 24


def position(n):
    depth = n // 8
    me = lax.axis_index("fsdp")
    return depth, me // 8, (me // 4) % 2, (me // 2) % 2, me % 2


def device_at(z, y, x, c):
    return ((z * 2 + y) * 2 + x) * 2 + c


def greet(partners):
    barrier = pltpu.get_barrier_semaphore()
    for device in partners:
        pl.semaphore_signal(barrier, inc=1, device_id=(device,), device_id_type=MESH)
    pl.semaphore_wait(barrier, len(partners))


def remote(src, dst, send, recv, device):
    return pltpu.make_async_remote_copy(
        src_ref=src,
        dst_ref=dst,
        send_sem=send,
        recv_sem=recv,
        device_id=(device,),
        device_id_type=MESH,
    )


def gather_kernel(n, wide, proj, vec, wide_out, proj_out, vec_out, local, ssem, rsem):
    depth, z, y, x, c = position(n)
    z_peers = [device_at((z + d) % depth, y, x, c) for d in range(1, depth)]
    y_peer, x_peer = device_at(z, 1 - y, x, c), device_at(z, y, 1 - x, c)
    core_peer = device_at(z, y, x, 1 - c)
    greet(z_peers + [y_peer, x_peer, core_peer])
    sends = []
    count = [0]

    def push(src, dst, device, landed):
        k = count[0]
        count[0] = k + 1
        copy = remote(src, dst, ssem.at[k], rsem.at[k], device)
        copy.start()
        sends.append(copy)
        return remote(landed, landed, ssem.at[k], rsem.at[k], device)

    own = [
        pltpu.make_async_copy(wide, wide_out.at[z, y, x, c], local.at[0]),
        pltpu.make_async_copy(proj, proj_out.at[z, y, x, c], local.at[1]),
        pltpu.make_async_copy(vec, vec_out.at[z, y, x, c], local.at[2]),
    ]
    for copy in own:
        copy.start()

    def wide_low(zi, p, q, ci):
        return wide_out.at[zi, p, q, ci, :, pl.ds(0, WIDE_A)]

    def wide_high(zi, p, q, ci):
        return wide_out.at[zi, q, p, ci, :, pl.ds(WIDE_A, wide.shape[1] - WIDE_A)]

    def proj_at(zi, p, q, ci):
        return proj_out.at[zi, q, p, ci]

    def vec_at(zi, p, q, ci):
        return vec_out.at[zi, q, p, ci]

    yx = (y, x, y_peer, x_peer)
    xy = (x, y, x_peer, y_peer)
    streams = [
        (wide.at[:, pl.ds(0, WIDE_A)], wide_low, yx),
        (wide.at[:, pl.ds(WIDE_A, wide.shape[1] - WIDE_A)], wide_high, xy),
        (proj, proj_at, xy),
        (vec, vec_at, xy),
    ]
    every = pl.ds(0, depth)
    from_z = [[] for _ in streams]
    from_first = [[] for _ in streams]
    from_second = [[] for _ in streams]
    from_far = [[] for _ in streams]
    from_core = []
    for d in range(1, depth):
        for s, (mine, at, (p, q, _, _)) in enumerate(streams):
            from_z[s].append(
                push(mine, at(z, p, q, c), z_peers[d - 1], at((z + depth - d) % depth, p, q, c))
            )
    for s, (mine, at, (p, q, first, second)) in enumerate(streams):
        from_first[s].append(push(mine, at(z, p, q, c), first, at(z, 1 - p, q, c)))
        from_second[s].append(push(mine, at(z, p, q, c), second, at(z, p, 1 - q, c)))
    for copy in own:
        copy.wait()
    for d in range(1, depth):
        zi = (z + depth - d) % depth
        for s, (mine, at, (p, q, first, second)) in enumerate(streams):
            from_z[s][d - 1].wait_recv()
            here = at(zi, p, q, c)
            from_first[s].append(push(here, here, first, at(zi, 1 - p, q, c)))
            from_second[s].append(push(here, here, second, at(zi, p, 1 - q, c)))
    for mine, at, (p, q, _, _) in streams:
        here = at(every, p, q, c)
        from_core.append(push(here, here, core_peer, at(every, p, q, 1 - c)))
    for d in range(depth):
        zi = (z + depth - d) % depth
        for s, (mine, at, (p, q, first, second)) in enumerate(streams):
            from_first[s][d].wait_recv()
            here = at(zi, 1 - p, q, c)
            from_far[s].append(push(here, here, second, at(zi, 1 - p, 1 - q, c)))
    for mine, at, (p, q, _, _) in streams:
        here = at(every, 1 - p, q, c)
        from_core.append(push(here, here, core_peer, at(every, 1 - p, q, 1 - c)))
    for s, (mine, at, (p, q, _, _)) in enumerate(streams):
        for d in range(depth):
            from_second[s][d].wait_recv()
        here = at(every, p, 1 - q, c)
        from_core.append(push(here, here, core_peer, at(every, p, 1 - q, 1 - c)))
    for s, (mine, at, (p, q, _, _)) in enumerate(streams):
        for d in range(depth):
            from_far[s][d].wait_recv()
        here = at(every, 1 - p, 1 - q, c)
        from_core.append(push(here, here, core_peer, at(every, 1 - p, 1 - q, 1 - c)))
    for copy in from_core:
        copy.wait_recv()
    for copy in sends:
        copy.wait_send()


def gather_all(n, wide, proj, vec):
    depth = n // 8
    lead = (depth, 2, 2, 2)
    copies = 4 * (depth - 1 + 3 * depth + 4)
    out = tuple(jax.ShapeDtypeStruct(lead + part.shape, part.dtype) for part in (wide, proj, vec))
    space = pl.BlockSpec(memory_space=pl.ANY)
    wide_out, proj_out, vec_out = pl.pallas_call(
        functools.partial(gather_kernel, n),
        out_shape=out,
        in_specs=[space] * 3,
        out_specs=(space,) * 3,
        scratch_shapes=[
            pltpu.SemaphoreType.DMA((3,)),
            pltpu.SemaphoreType.DMA((copies,)),
            pltpu.SemaphoreType.DMA((copies,)),
        ],
        compiler_params=pltpu.CompilerParams(collective_id=0, has_side_effects=True),
    )(wide, proj, vec)
    return (
        wide_out.reshape(n * wide.shape[0], wide.shape[1]),
        proj_out.reshape(n * proj.shape[0], proj.shape[1]),
        vec_out.reshape(n, *vec.shape),
    )


def scatter_kernel(
    n,
    in_a,
    att_a,
    sec_a,
    sec_b,
    hid_b,
    qkv_g,
    res_g,
    pre_g,
    cot,
    vec,
    wide_out,
    proj_out,
    vec_out,
    given,
    kept,
    land_core,
    land_second,
    land_third,
    land_z,
    vec_kept,
    vec_core,
    vec_second,
    vec_third,
    vec_z,
    ssem,
    rsem,
):
    depth, z, y, x, c = position(n)
    z_devices = [device_at((z + d) % depth, y, x, c) for d in range(1, depth)]
    y_peer, x_peer = device_at(z, 1 - y, x, c), device_at(z, y, 1 - x, c)
    core_peer = device_at(z, y, x, 1 - c)
    greet(z_devices + [y_peer, x_peer, core_peer])
    second_peer = (x_peer, y_peer)
    third_peer = (y_peer, x_peer)
    spots = ((x, y), (y, x))
    sends = []
    count = [24]

    def push(src, dst, device):
        k = count[0]
        count[0] = k + 1
        copy = remote(src, dst, ssem.at[k], rsem.at[k], device)
        copy.start()
        sends.append(copy)
        return copy

    vec_copy = push(vec.at[1 - c], vec_core, core_peer)

    def product(left, right):
        return jnp.dot(left, right, preferred_element_type=jnp.float32)

    def block(left, right):
        return product(left, right).reshape(depth, GROUP, D)

    def fill(k, s, half, t, target):
        i = (spots[s][0] + 1 - t // 2) % 2
        j = (spots[s][1] + 1 - t % 2) % 2
        if s == 0:
            left = in_a[half, i, j]
            if k == 0:
                pair = (block(left, qkv_g[:, 0:D]), block(left, qkv_g[:, D : 2 * D]))
            elif k == 1:
                pair = (
                    block(left, qkv_g[:, 2 * D : 3 * D]),
                    block(att_a[half, i, j], res_g[...]),
                )
            else:
                left = sec_a[half, i, j]
                pair = (block(left, pre_g[:, 0:D]), block(left, pre_g[:, D : 2 * D]))
            value = jnp.concatenate(pair, axis=1)
        elif k == 0:
            left = sec_b[half, i, j]
            value = jnp.concatenate(
                (block(left, pre_g[:, 2 * D : 3 * D]), block(left, pre_g[:, 3 * D : 4 * D])), axis=1
            )
        else:
            value = product(hid_b[k - 1, half, i, j], cot[...]).reshape(depth, 2 * GROUP, D)
        target[...] = value.astype(jnp.bfloat16)

    def core_copy(k, s, t):
        q = (k * 2 + s) * 4 + t
        return remote(
            given.at[k, s, t], land_core.at[k, s, t], ssem.at[q], rsem.at[q], core_peer
        )

    def multiply(k):
        def give(t, carry):
            for s in range(2):
                fill(k, s, 1 - c, t, given.at[k, s, t])
                core_copy(k, s, t).start()
            return carry

        def keep(t, carry):
            for s in range(2):
                fill(k, s, c, t, kept.at[k, s, t])
            return carry

        lax.fori_loop(0, 4, give, 0)
        lax.fori_loop(0, 4, keep, 0)

    def merge(target, landed):
        def step(k, carry):
            target[k] = (
                target[k].astype(jnp.float32) + landed[k].astype(jnp.float32)
            ).astype(jnp.bfloat16)
            return carry

        lax.fori_loop(0, depth, step, 0)

    second, third, last = {}, {}, {}

    def stage_second(k):
        for t in range(4):
            for s in range(2):
                core_copy(k, s, t).wait_recv()
                merge(kept.at[k, s, t], land_core.at[k, s, t])
                if t < 2:
                    second[k, s, t] = push(
                        kept.at[k, s, t], land_second.at[k, s, t], second_peer[s]
                    )

    def stage_third(k):
        for t in range(2):
            for s in range(2):
                second[k, s, t].wait_recv()
                merge(kept.at[k, s, 2 + t], land_second.at[k, s, t])
                if t == 0:
                    third[k, s] = push(kept.at[k, s, 2], land_third.at[k, s], third_peer[s])

    def stage_last(k):
        for s in range(2):
            third[k, s].wait_recv()
            merge(kept.at[k, s, 3], land_third.at[k, s])
            last[k, s] = [
                push(kept.at[k, s, 3, (z + d) % depth], land_z.at[k, s, d - 1], z_devices[d - 1])
                for d in range(1, depth)
            ]

    def finish(k):
        for s in range(2):
            total = kept[k, s, 3, z].astype(jnp.float32)
            for d in range(depth - 1):
                last[k, s][d].wait_recv()
                total += land_z[k, s, d].astype(jnp.float32)
            for b in range(2):
                rows = total[b * GROUP : (b + 1) * GROUP]
                if s == 1 and k > 0:
                    first = ((k - 1) * 2 + b) * GROUP
                    proj_out[first : first + GROUP] = rows
                else:
                    column = (6 * s + 2 * k + b) * D
                    wide_out[:, column : column + D] = rows

    multiply(0)
    stage_second(0)
    vec_copy.wait_recv()
    vec_kept[...] = vec[c] + vec_core[...]
    vec_copy = push(vec_kept.at[1 - x], vec_second, x_peer)
    multiply(1)
    stage_second(1)
    stage_third(0)
    vec_copy.wait_recv()
    vec_kept[x] += vec_second[...]
    vec_copy = push(vec_kept.at[x, 1 - y], vec_third, y_peer)
    multiply(2)
    stage_second(2)
    stage_last(0)
    stage_third(1)
    vec_copy.wait_recv()
    vec_kept[x, y] += vec_third[...]
    vec_last = [
        push(vec_kept.at[x, y, (z + d) % depth], vec_z.at[d - 1], z_devices[d - 1])
        for d in range(1, depth)
    ]
    stage_last(1)
    stage_third(2)
    stage_last(2)
    total = vec_kept[x, y, z]
    for d in range(depth - 1):
        vec_last[d].wait_recv()
        total += vec_z[d]
    vec_out[...] = total
    for k in range(3):
        finish(k)
    for k in range(3):
        for s in range(2):
            for t in range(4):
                core_copy(k, s, t).wait_send()
    for copy in sends:
        copy.wait_send()


def by_owner(rows, n, order):
    depth = n // 8
    size = rows.shape[0] // n
    names = {"y": 1, "x": 2, "c": 3}
    split = rows.reshape(depth, 2, 2, 2, size, *rows.shape[1:])
    rest = tuple(range(4, split.ndim))
    return split.transpose(*(names[k] for k in order), 0, *rest)


def scatter_all(n, first_in, attended, second_in, hidden, qkv_grad, resid_half, pre_grad, cot, vec):
    depth = n // 8

    def left(rows, order):
        ordered = by_owner(rows.T, n, order)
        return ordered.reshape(2, 2, 2, -1, rows.shape[0])

    dtype = jnp.bfloat16
    unit = (depth, 2 * GROUP, D)
    tile = vec.shape[1:]
    copies = 24 + 6 * (2 + 1 + depth - 1) + 3 + depth - 1
    space = pl.BlockSpec(memory_space=pltpu.VMEM)
    return pl.pallas_call(
        functools.partial(scatter_kernel, n),
        out_shape=(
            jax.ShapeDtypeStruct((GROUP, 8 * D), jnp.float32),
            jax.ShapeDtypeStruct((4 * GROUP, D), jnp.float32),
            jax.ShapeDtypeStruct(tile, jnp.float32),
        ),
        in_specs=[space] * 10,
        out_specs=(space,) * 3,
        scratch_shapes=[
            pltpu.VMEM((3, 2, 4) + unit, dtype),
            pltpu.VMEM((3, 2, 4) + unit, dtype),
            pltpu.VMEM((3, 2, 4) + unit, dtype),
            pltpu.VMEM((3, 2, 2) + unit, dtype),
            pltpu.VMEM((3, 2) + unit, dtype),
            pltpu.VMEM((3, 2, depth - 1, 2 * GROUP, D), dtype),
            pltpu.VMEM((2, 2, depth) + tile, jnp.float32),
            pltpu.VMEM((2, 2, depth) + tile, jnp.float32),
            pltpu.VMEM((2, depth) + tile, jnp.float32),
            pltpu.VMEM((depth,) + tile, jnp.float32),
            pltpu.VMEM((depth - 1,) + tile, jnp.float32),
            pltpu.SemaphoreType.DMA((copies,)),
            pltpu.SemaphoreType.DMA((copies,)),
        ],
        compiler_params=pltpu.CompilerParams(
            collective_id=1, has_side_effects=True, vmem_limit_bytes=52 * 2**20
        ),
    )(
        left(first_in, "cxy"),
        left(attended, "cxy"),
        left(second_in, "cxy"),
        left(second_in, "cyx"),
        by_owner(hidden.T, n, "cyx")
        .reshape(2, 2, 2, depth, 2, 2 * GROUP, hidden.shape[0])
        .transpose(4, 0, 1, 2, 3, 5, 6)
        .reshape(2, 2, 2, 2, depth * 2 * GROUP, hidden.shape[0]),
        qkv_grad,
        resid_half,
        pre_grad,
        cot,
        by_owner(vec, n, "cxy").reshape(2, 2, 2, depth, *tile),
    )


def to_tile(rows):
    flat = rows.reshape(rows.shape[0], -1)
    return jnp.pad(flat, ((0, 0), (0, 1024 - flat.shape[1]))).reshape(rows.shape[0], 8, 128)


def from_tile(tiles, rows, columns):
    return tiles.reshape(tiles.shape[0], 1024)[:, : rows * columns].reshape(-1, rows, columns)


def body(
    tokens,
    seq_lengths,
    cotangent,
    wide_weights,
    proj_weights,
    vector_params,
    wide_moments,
    proj_moments,
    vector_moments,
):
    shards = (
        wide_weights.astype(jnp.bfloat16),
        proj_weights.astype(jnp.bfloat16),
        vector_params.astype(jnp.bfloat16),
    )
    devices = lax.axis_size("fsdp")
    direct = wide_weights.shape[0] == GROUP and devices % 8 == 0
    vector_rows, vector_columns = vector_params.shape
    if direct:
        wide_full, proj_full, vector_tiles = gather_all(
            devices, shards[0], shards[1], to_tile(shards[2].astype(jnp.float32)[None])[0]
        )
        vector_full = (
            from_tile(vector_tiles, vector_rows, vector_columns)
            .transpose(1, 0, 2)
            .reshape(vector_rows, devices * vector_columns)
        )
    else:
        wide_full, proj_full, vector_full = (
            lax.all_gather(shards[0], "fsdp", axis=0, tiled=True),
            lax.all_gather(shards[1], "fsdp", axis=0, tiled=True),
            lax.all_gather(shards[2], "fsdp", axis=1, tiled=True),
        )
    vectors = vector_full.astype(jnp.float32)
    row_count = tokens.shape[0]
    allowed = allowed_pairs(seq_lengths[0], row_count)
    ratio = FF // D
    local_rows = wide_weights.shape[0]
    unscale = math.sqrt(lax.axis_size("fsdp") * row_count)
    gain_one, shift_one, query_bias, value_bias = (vectors[0], vectors[1], vectors[2], vectors[3])
    out_bias, gain_two, shift_two, proj_bias = (vectors[4], vectors[5], vectors[6], vectors[7])
    fc_bias = vectors[8:].reshape(FF)
    token_float = tokens.astype(jnp.float32)
    first_norm, normed_one, inverse_one = norm_forward(token_float, gain_one, shift_one)
    first_in = first_norm.astype(jnp.bfloat16)
    qkv_bias = jnp.concatenate([query_bias, jnp.zeros_like(query_bias), value_bias])
    qkv_half = (
        jnp.dot(first_in, wide_full[:, : 3 * D], preferred_element_type=jnp.float32) + qkv_bias
    ).astype(jnp.bfloat16)
    queries = qkv_half[:, :D]
    key_rows = qkv_half[:, D : 2 * D]
    value_rows = qkv_half[:, 2 * D :]
    attended, logsum = attention_forward(queries, key_rows, value_rows, allowed)
    residual = (
        token_float
        + jnp.dot(attended, wide_full[:, 3 * D : 4 * D], preferred_element_type=jnp.float32)
        + out_bias
    )
    second_norm, normed_two, inverse_two = norm_forward(residual, gain_two, shift_two)
    second_in = second_norm.astype(jnp.bfloat16)
    before_act = (
        jnp.dot(second_in, wide_full[:, 4 * D :], preferred_element_type=jnp.float32) + fc_bias
    )
    value_part, slope_part = gelu_parts(before_act)
    hidden = value_part.astype(jnp.bfloat16)
    block_output = (
        residual + jnp.dot(hidden, proj_full, preferred_element_type=jnp.float32) + proj_bias
    ).astype(jnp.bfloat16)
    backward_wide, backward_proj, vector_again = wide_full, proj_full, vector_full
    backward_vectors = vector_again.astype(jnp.float32)
    qkv_back = backward_wide[:, : 3 * D]
    out_back = backward_wide[:, 3 * D : 4 * D]
    fc_back = backward_wide[:, 4 * D :]
    cot_float = cotangent.astype(jnp.float32)
    proj_bias_grad = jnp.sum(cot_float, axis=0)
    hidden_grad = jnp.einsum(
        "td,fd->tf", cotangent, backward_proj, preferred_element_type=jnp.float32
    )
    pre_grad = (hidden_grad * slope_part).astype(jnp.bfloat16)
    fc_bias_grad = jnp.sum(pre_grad, axis=0, dtype=jnp.float32)
    second_grad = jnp.einsum("tf,df->td", pre_grad, fc_back, preferred_element_type=jnp.float32)
    resid_norm_grad, gain_two_grad, shift_two_grad = norm_backward(
        second_grad, normed_two, inverse_two, backward_vectors[5]
    )
    resid_grad = cot_float + resid_norm_grad
    mlp_vectors = jnp.concatenate(
        [
            jnp.stack([gain_two_grad, shift_two_grad, proj_bias_grad]),
            fc_bias_grad.reshape(ratio, D),
        ],
        axis=0,
    )
    resid_half = resid_grad.astype(jnp.bfloat16)
    out_bias_grad = jnp.sum(resid_grad, axis=0)
    attended_grad = jnp.einsum(
        "te,de->td", resid_half, out_back, preferred_element_type=jnp.float32
    ).astype(jnp.bfloat16)
    qkv_grad = attention_backward(queries, key_rows, value_rows, allowed, logsum, attended_grad)
    query_bias_grad = jnp.sum(qkv_grad[:, :D], axis=0, dtype=jnp.float32)
    value_bias_grad = jnp.sum(qkv_grad[:, 2 * D :], axis=0, dtype=jnp.float32)
    first_grad = jnp.einsum("tc,dc->td", qkv_grad, qkv_back, preferred_element_type=jnp.float32)
    token_norm_grad, gain_one_grad, shift_one_grad = norm_backward(
        first_grad, normed_one, inverse_one, backward_vectors[0]
    )
    tokens_grad = (resid_grad + token_norm_grad).astype(jnp.bfloat16)
    attn_vectors = jnp.stack(
        [gain_one_grad, shift_one_grad, query_bias_grad, value_bias_grad, out_bias_grad]
    )
    vector_terms = jnp.concatenate([attn_vectors, mlp_vectors], axis=0)
    if direct:
        owned = vector_terms.reshape(vector_rows, devices, vector_columns).transpose(1, 0, 2)
        wide_grad, proj_grad, vector_tile = scatter_all(
            devices,
            first_in,
            attended,
            second_in,
            hidden,
            qkv_grad,
            resid_half,
            pre_grad,
            cotangent,
            to_tile(owned),
        )
        vector_grad = from_tile(vector_tile[None], vector_rows, vector_columns)[0]
    else:
        fc_part = column_term(second_in, pre_grad)
        proj_part = column_term(hidden, cotangent).reshape(
            local_rows * lax.axis_size("fsdp"), ratio * D
        )
        qkv_part = column_term(first_in, qkv_grad)
        out_part = column_term(attended, resid_half)
        joined_shard = lax.psum_scatter(
            jnp.concatenate(
                [
                    jnp.concatenate([qkv_part, out_part], axis=1),
                    jnp.concatenate([fc_part, proj_part], axis=1),
                ],
                axis=1,
            ),
            "fsdp",
            scatter_dimension=0,
            tiled=True,
        )
        wide_grad = joined_shard[:, : 4 * D + FF]
        proj_grad = joined_shard[:, 4 * D + FF :].reshape(local_rows * ratio, D)
        vector_grad = lax.psum_scatter(vector_terms, "fsdp", scatter_dimension=1, tiled=True)
    wide_new, wide_moments_new = adam_update(
        wide_weights, wide_moments, wide_grad, rate_matrix, weight_decay, unscale
    )
    proj_new, proj_moments_new = adam_update(
        proj_weights, proj_moments, proj_grad, rate_matrix, weight_decay, unscale
    )
    vector_new, vector_moments_new = adam_update(
        vector_params, vector_moments, vector_grad, rate_vector, 0.0, unscale
    )
    return (
        block_output,
        tokens_grad,
        wide_grad,
        proj_grad,
        vector_grad,
        wide_new,
        proj_new,
        vector_new,
        wide_moments_new,
        proj_moments_new,
        vector_moments_new,
    )


def solution(mesh):
    placed = (
        P("fsdp", None),
        P("fsdp", None),
        P("fsdp", None),
        P("fsdp", None),
        P("fsdp", None),
        P(None, "fsdp"),
        P(None, "fsdp", None),
        P(None, "fsdp", None),
        P(None, None, "fsdp"),
    )
    return jax.shard_map(
        body,
        mesh=mesh,
        in_specs=placed,
        out_specs=(
            P("fsdp", None),
            P("fsdp", None),
            P("fsdp", None),
            P("fsdp", None),
            P(None, "fsdp"),
            P("fsdp", None),
            P("fsdp", None),
            P(None, "fsdp"),
            P(None, "fsdp", None),
            P(None, "fsdp", None),
            P(None, None, "fsdp"),
        ),
        check_vma=False,
    )
```

```python
import functools
import math
import types

import jax
import jax.numpy as jnp
from jax import lax
from jax.experimental import pallas as pl
from jax.experimental.pallas import tpu as pltpu
from jax.sharding import PartitionSpec as P

D = 768
H = 12
HD = 64
FF = 3072
STEP = 2


norm_eps = 1e-05
beta_one = 0.9
beta_two = 0.95
adam_eps = 1e-08
rate_matrix = 0.02
rate_vector = 0.2
weight_decay = 0.1
gelu_coeff = 0.7978845608028654
masked_score = -1e30


def norm_forward(values, gain_row, offset):
    center = values - jnp.mean(values, axis=1, keepdims=True)
    variance = jnp.mean(center * center, axis=1, keepdims=True)
    inverse = lax.rsqrt(variance + norm_eps)
    normed = center * inverse
    return (normed * gain_row + offset, normed, inverse)


def norm_backward(upstream, normed, inverse, gain_row):
    scaled = upstream * gain_row
    mean_term = jnp.mean(scaled, axis=1, keepdims=True)
    proj_term = jnp.mean(scaled * normed, axis=1, keepdims=True)
    input_grad = inverse * (scaled - mean_term - normed * proj_term)
    return (input_grad, jnp.sum(upstream * normed, axis=0), jnp.sum(upstream, axis=0))


def gelu_parts(before):
    inner_arg = gelu_coeff * (before + 0.044715 * before * before * before)
    tangent = jnp.tanh(inner_arg)
    value_part = 0.5 * before * (1.0 + tangent)
    slope_part = 0.5 * (1.0 + tangent) + 0.5 * before * (1.0 - tangent * tangent) * gelu_coeff * (
        1.0 + 3.0 * 0.044715 * before * before
    )
    return (value_part, slope_part)


def allowed_pairs(length_row, row_count):
    order = jnp.arange(length_row.shape[0], dtype=jnp.int32)
    bounds = jnp.sum(jnp.where(order[None, :] <= order[:, None], length_row[None, :], 0), axis=1)
    position = jnp.arange(row_count, dtype=jnp.int32)
    segment = jnp.sum((position[:, None] >= bounds[None, :]).astype(jnp.int32), axis=1)
    return (segment[:, None] == segment[None, :]) & (position[None, :] <= position[:, None])


def head_view(matrix):
    return matrix.reshape(matrix.shape[0], H, HD)


def score_table(queries, key_rows, allowed):
    scale_factor = 1.0 / math.sqrt(HD)
    scores = (
        jnp.einsum(
            "qhd,khd->hqk",
            head_view(queries),
            head_view(key_rows),
            preferred_element_type=jnp.float32,
        )
        * scale_factor
    )
    return jnp.where(allowed[None, :, :], scores, masked_score)


def attention_forward(queries, key_rows, value_rows, allowed):
    scores = score_table(queries, key_rows, allowed)
    highest = jnp.max(scores, axis=2, keepdims=True)
    logsum = highest + jnp.log(jnp.sum(jnp.exp(scores - highest), axis=2, keepdims=True))
    weights = jnp.exp(scores - logsum).astype(jnp.bfloat16)
    mixed = jnp.einsum(
        "hqk,khd->qhd", weights, head_view(value_rows), preferred_element_type=jnp.float32
    )
    return (mixed.reshape(queries.shape[0], D).astype(jnp.bfloat16), logsum)


def attention_backward(queries, key_rows, value_rows, allowed, logsum, upstream):
    scale_factor = 1.0 / math.sqrt(HD)
    scores = score_table(queries, key_rows, allowed)
    probs = jnp.exp(scores - logsum)
    rounded = probs.astype(jnp.bfloat16)
    grad_heads = head_view(upstream)
    value_grad = jnp.einsum("hqk,qhd->khd", rounded, grad_heads, preferred_element_type=jnp.float32)
    prob_grad = jnp.einsum(
        "qhd,khd->hqk", grad_heads, head_view(value_rows), preferred_element_type=jnp.float32
    )
    delta_row = jnp.sum(probs * prob_grad, axis=2, keepdims=True)
    score_grad = (probs * (prob_grad - delta_row) * scale_factor).astype(jnp.bfloat16)
    query_grad = jnp.einsum(
        "hqk,khd->qhd", score_grad, head_view(key_rows), preferred_element_type=jnp.float32
    )
    key_grad = jnp.einsum(
        "hqk,qhd->khd", score_grad, head_view(queries), preferred_element_type=jnp.float32
    )
    row_total = queries.shape[0]
    joined = jnp.concatenate(
        [
            query_grad.reshape(row_total, D),
            key_grad.reshape(row_total, D),
            value_grad.reshape(row_total, D),
        ],
        axis=1,
    )
    return joined.astype(jnp.bfloat16)


def adam_update(weights, moments, gradient, rate, decay_rate, unscale):
    scaled_grad = gradient / unscale
    first_moment = beta_one * moments[0] + (1.0 - beta_one) * scaled_grad
    second_moment = beta_two * moments[1] + (1.0 - beta_two) * scaled_grad * scaled_grad
    corrected_first = first_moment / (1.0 - beta_one**STEP)
    corrected_second = second_moment / (1.0 - beta_two**STEP)
    updated = weights - rate * (
        corrected_first / (jnp.sqrt(corrected_second) + adam_eps) + decay_rate * weights
    )
    return (updated, jnp.stack([first_moment, second_moment]))


def column_term(left, right):
    return jnp.einsum("tc,te->ce", left, right, preferred_element_type=jnp.float32)


MESH = pl.DeviceIdType.MESH
GROUP = 24


def position(n):
    depth = n // 8
    me = lax.axis_index("fsdp")
    return depth, me // 8, (me // 4) % 2, (me // 2) % 2, me % 2


def device_at(z, y, x, c):
    return ((z * 2 + y) * 2 + x) * 2 + c


def greet(partners):
    barrier = pltpu.get_barrier_semaphore()
    for device in partners:
        pl.semaphore_signal(barrier, inc=1, device_id=(device,), device_id_type=MESH)
    pl.semaphore_wait(barrier, len(partners))


def remote(src, dst, send, recv, device):
    return pltpu.make_async_remote_copy(
        src_ref=src,
        dst_ref=dst,
        send_sem=send,
        recv_sem=recv,
        device_id=(device,),
        device_id_type=MESH,
    )


def product(left, right):
    return jnp.dot(left, right, preferred_element_type=jnp.float32)


def product_nt(left, right):
    return lax.dot_general(
        left, right, (((1,), (1,)), ((), ())), preferred_element_type=jnp.float32
    )


def product_tn(left, right):
    return lax.dot_general(
        left, right, (((0,), (0,)), ((), ())), preferred_element_type=jnp.float32
    )


TOK = 128
UNIT = 2 * GROUP
W1 = 4 * D + 256
W1_HALF = W1 // 2
W1_FIRST = 1024
F_HALF = FF // 2
F_FIRST = 1024
P_ROWS = FF // 32
P_FIRST = 64
ROWS_OF = (2 * P_ROWS, UNIT, UNIT)
FIRST_OF = (256, 1024, 1024)
WIDTH_OF = (384, 1536, 1536)


def scratch_of(depth):
    half, full = jnp.bfloat16, jnp.float32

    def vmem(shape, dtype):
        return pltpu.VMEM(shape, dtype)

    lead = (depth, 2, 2)
    spaces = dict(
        ext=vmem((32, 4 * D + 256 + FF), half),
        ext_in=vmem((32, 4 * D + 256 + FF), half),
        w1=vmem(lead + (UNIT, W1), half),
        wf=vmem(lead + (UNIT, FF), half),
        wp=vmem(lead + (2 * P_ROWS, D), half),
        vecs=vmem((16, D + 128), full),
        normed=vmem((TOK, D), full),
        inverse=vmem((TOK, 128), full),
        normed2=vmem((TOK, D), full),
        inverse2=vmem((TOK, 128), full),
        allowed=vmem((TOK, TOK), full),
        window=vmem((GROUP, 256), full),
        qkv=vmem((TOK, 3 * D), half),
        probs=vmem((H, TOK, TOK), full),
        mixed=vmem((TOK, D), half),
        resid=vmem((TOK, D), full),
        second=vmem((TOK, D), half),
        slope=vmem((TOK, FF), full),
        hidden=vmem((TOK, FF), half),
        pre=vmem((TOK, FF), half),
        up=vmem((TOK, D), half),
        qg=vmem((TOK, 3 * D), half),
        a1t=vmem(lead + (UNIT, 2 * TOK), half),
        att=vmem(lead + (UNIT, 2 * TOK), half),
        a2t=vmem(lead + (UNIT, 2 * TOK), half),
        hidt=vmem(lead + (2 * P_ROWS, 2 * TOK), half),
        rhsp=vmem((2 * TOK, 384), half),
        rhsf=vmem((2 * TOK, F_HALF), half),
        rhs1=vmem((2 * TOK, 4 * 384), half),
        vterm=vmem((16, D), full),
        vsend=vmem((4, 16, 384), full),
        vrecv=vmem((4, 16, 384), full),
        vz=vmem((depth - 1, 16, 384), full),
    )
    parts = []
    for k in range(3):
        rows, first, width = ROWS_OF[k], FIRST_OF[k], WIDTH_OF[k]
        rest = width - first
        parts.append(
            dict(
                give_a=vmem((depth, 2, rows, first), half),
                land_a=vmem((depth, 2, rows, first), half),
                keep_a=vmem((depth, 2, rows, first), full),
                give_b=vmem((depth, 2, rows, rest), half),
                land_b=vmem((depth, 2, rows, rest), half),
                keep_b=vmem((depth, 2, rows, rest), full),
                sa2=vmem((depth, rows, first), half),
                ra2=vmem((depth, rows, first), half),
                sa3=vmem((depth, rows, first), half),
                ra3=vmem((depth - 1, rows, first), half),
                sb2=vmem((depth, 2, rows, rest), half),
                rb2=vmem((depth - 1, 2, rows, rest), half),
                sb3=vmem((rows, rest), half),
                rb3=vmem((rows, rest), half),
                fin=vmem((rows, width), full),
                rfin=vmem((rows // 2, width), full),
            )
        )
    return spaces, parts


COPIES = 203


def block_kernel(n, names, tok, lens, cot, wide, proj, vec, block_out, tok_out, wide_out, proj_out, vec_out, *refs):
    names, part_names = names
    ssem, rsem = refs[0], refs[1]
    r = types.SimpleNamespace(**dict(zip(names, refs[2:])))
    part_refs = []
    for k in range(3):
        first = 2 + len(names) + k * len(part_names)
        part_refs.append(types.SimpleNamespace(**dict(zip(part_names, refs[first:]))))
    depth, z, y, x, c = position(n)
    z_devices = [device_at((z + d) % depth, y, x, c) for d in range(1, depth)]
    yp, xp = device_at(z, 1 - y, x, c), device_at(z, y, 1 - x, c)
    cp = device_at(z, y, x, 1 - c)
    half, full = jnp.bfloat16, jnp.float32
    sends = []
    count = [0]

    def push(src, dst, device, landed=None):
        k = count[0]
        count[0] = k + 1
        copy = remote(src, dst, ssem.at[k], rsem.at[k], device)
        copy.start()
        sends.append(copy)
        landed = dst if landed is None else landed
        return remote(landed, landed, ssem.at[k], rsem.at[k], device)

    def lanes(start, size):
        return pl.ds(pl.multiple_of(start, 128), size)

    wide_now = wide[...].astype(half).astype(full)
    r.window[...] = jnp.zeros((GROUP, 256), full)
    r.window[0 : vec.shape[0], 0 : vec.shape[1]] = vec[...]
    shift = lax.rem(lax.axis_index("fsdp") * vec.shape[1], 128)
    vec_now = pltpu.roll(r.window[...], shift, 1)
    r.ext[0:GROUP, 0 : 4 * D] = wide_now[:, 0 : 4 * D].astype(half)
    r.ext[0:GROUP, 4 * D : W1] = vec_now.astype(half)
    r.ext[0:GROUP, W1:] = wide_now[:, 4 * D :].astype(half)
    r.ext[GROUP:, :] = jnp.zeros((32 - GROUP, W1 + FF), half)
    r.wp[z, y, x, pl.ds(pl.multiple_of(c * P_ROWS, 32), P_ROWS), :] = proj[...].astype(half)
    greet(z_devices + [yp, xp, cp])
    ext_copy = push(r.ext, r.ext_in, cp)

    def w1_at(s):
        start = c * W1_HALF + (W1_FIRST if s else 0)
        size = W1_HALF - W1_FIRST if s else W1_FIRST
        return lambda zi, yi, xi: r.w1.at[zi, yi, xi, :, lanes(start, size)]

    def wf_at(s):
        start = c * F_HALF + (F_FIRST if s else 0)
        size = F_HALF - F_FIRST if s else F_FIRST
        return lambda zi, yi, xi: r.wf.at[zi, yi, xi, :, lanes(start, size)]

    def wp_at(s):
        start = c * P_ROWS + (P_FIRST if s else 0)
        size = P_ROWS - P_FIRST if s else P_FIRST
        return lambda zi, yi, xi: r.wp.at[zi, yi, xi, pl.ds(pl.multiple_of(start, 32), size), :]

    every, both = pl.ds(0, depth), pl.ds(0, 2)

    def zat(d):
        return (z + depth - d) % depth

    class Gather:
        def __init__(self, a, b, own):
            self.a, self.b, self.own = a, b, own
            self.cores = []

        def core(self, ref, landed):
            self.cores.append((ref, landed))

        def start(self):
            a, b = self.a, self.b
            mine_a, mine_b = a(z, y, x), b(z, y, x)
            self.by = push(mine_b, mine_b, yp, b(z, 1 - y, x))
            self.az, self.bz, self.ax, self.ay, self.bx = [None], [None], [], [], []
            self.ax.append(push(mine_a, mine_a, xp, a(z, y, 1 - x)))
            self.ay.append(push(mine_a, mine_a, yp, a(z, 1 - y, x)))
            self.bx.append(push(mine_b, mine_b, xp, b(z, y, 1 - x)))
            self.done = []
            if self.own:
                self.done.append(push(mine_a, mine_a, cp, OWN_A(z, y, x)))
                self.done.append(push(mine_b, mine_b, cp, OWN_B(z, y, x)))

        def start_z(self):
            a, b = self.a, self.b
            mine_a, mine_b = a(z, y, x), b(z, y, x)
            for d in range(1, depth):
                self.az.append(push(mine_a, mine_a, z_devices[d - 1], a(zat(d), y, x)))
            for d in range(1, depth):
                self.bz.append([push(mine_b, mine_b, z_devices[d - 1], b(zat(d), y, x))])

        def first(self):
            b = self.b
            self.by.wait_recv()
            got = b(z, 1 - y, x)
            for d in range(1, depth):
                self.bz[d].append(push(got, got, z_devices[d - 1], b(zat(d), 1 - y, x)))
            self.bx.append(push(got, got, xp, b(z, 1 - y, 1 - x)))
            self.give(b, (z, 1 - y, x))

        def give(self, at, where):
            ref = at(*where)
            self.done.append(push(ref, ref, cp, (PEER_A if at is self.a else PEER_B)[id(self)](*where)))

        def near(self, d):
            a = self.a
            self.az[d].wait_recv()
            got = a(zat(d), y, x)
            self.ax.append(push(got, got, xp, a(zat(d), y, 1 - x)))
            self.ay.append(push(got, got, yp, a(zat(d), 1 - y, x)))
            self.give(a, (zat(d), y, x))

        def side(self, d):
            a = self.a
            self.ax[d].wait_recv()
            got = a(zat(d), y, 1 - x)
            self.ay.append(push(got, got, yp, a(zat(d), 1 - y, 1 - x)))

        def side_done(self):
            self.give(self.a, (every, y, 1 - x))

        def deep(self, d):
            b = self.b
            for k, yi in ((0, y), (1, 1 - y)):
                self.bz[d][k].wait_recv()
                got = b(zat(d), yi, x)
                self.bx.append(push(got, got, xp, b(zat(d), yi, 1 - x)))
            self.give(b, (zat(d), both, x))

        def last(self):
            for copy in self.bx:
                copy.wait_recv()
            self.give(self.b, (every, both, 1 - x))
            for copy in self.ay:
                copy.wait_recv()
            self.give(self.a, (every, 1 - y, both))

        def finish(self):
            for copy in self.done:
                copy.wait_recv()

    PEER_A, PEER_B = {}, {}

    def peer_at(ref, cut, start_of, size):
        start = start_of(1 - c)
        if cut == "lanes":
            return lambda zi, yi, xi: ref.at[zi, yi, xi, :, lanes(start, size)]
        return lambda zi, yi, xi: ref.at[zi, yi, xi, pl.ds(pl.multiple_of(start, 32), size), :]

    g1 = Gather(w1_at(0), w1_at(1), False)
    gf = Gather(wf_at(0), wf_at(1), False)
    gp = Gather(wp_at(0), wp_at(1), True)
    for g, ref, cut, whole, cut_at in (
        (g1, r.w1, "lanes", W1_HALF, W1_FIRST),
        (gf, r.wf, "lanes", F_HALF, F_FIRST),
        (gp, r.wp, "rows", P_ROWS, P_FIRST),
    ):
        PEER_A[id(g)] = peer_at(ref, cut, lambda k, w=whole: k * w, cut_at)
        PEER_B[id(g)] = peer_at(ref, cut, lambda k, w=whole, o=cut_at: k * w + o, whole - cut_at)
    OWN_A, OWN_B = PEER_A[id(gp)], PEER_B[id(gp)]

    token_float = tok[...].astype(full)
    center = token_float - jnp.mean(token_float, axis=1, keepdims=True)
    inverse = lax.rsqrt(jnp.mean(center * center, axis=1, keepdims=True) + norm_eps)
    r.normed[...] = center * inverse
    r.inverse[...] = jnp.broadcast_to(inverse, (TOK, 128))
    across = lax.broadcasted_iota(jnp.int32, (TOK, TOK), 1)
    down = lax.broadcasted_iota(jnp.int32, (TOK, TOK), 0)
    seg_across = jnp.zeros((TOK, TOK), jnp.int32)
    seg_down = jnp.zeros((TOK, TOK), jnp.int32)
    bound = 0
    for j in range(lens.shape[1]):
        bound = bound + lens[0, j]
        seg_across += (across >= bound).astype(jnp.int32)
        seg_down += (down >= bound).astype(jnp.int32)
    r.allowed[...] = ((seg_across == seg_down) & (across <= down)).astype(full)

    ext_copy.wait_recv()

    def assemble(target, start, size):
        for o in range(0, size, 512):
            w = min(512, size - o)
            mine = r.ext[:, start + o : start + o + w].astype(full)[:GROUP]
            theirs = r.ext_in[:, start + o : start + o + w].astype(full)[:GROUP]
            low = jnp.where(c == 0, mine, theirs)
            high = jnp.where(c == 0, theirs, mine)
            target[z, y, x, :, o : o + w] = jnp.concatenate([low, high], axis=0).astype(half)

    assemble(r.w1, 0, W1)
    g1.start()
    g1.start_z()
    assemble(r.wf, W1, FF)
    gf.start()
    gp.start()
    cot_copy = push(cot.at[:, lanes((1 - c) * 384, 384)], r.rhsp.at[pl.ds(TOK, TOK), :], cp)
    r.rhsp[0:TOK, :] = cot[:, lanes(c * 384, 384)]
    g1.first()
    gf.start_z()
    gf.first()
    gp.start_z()
    gp.first()
    g1.near(1)
    g1.side(0)
    g1.near(2)
    g1.side(1)
    g1.near(3)
    g1.side(2)
    g1.deep(1)
    g1.side(3)
    g1.side_done()
    g1.deep(2)
    g1.deep(3)
    gf.near(1)
    gf.side(0)
    g1.last()
    gf.near(2)
    g1.finish()

    r.vecs[...] = jnp.zeros((16, D + 128), full)
    for chip in range(n // 2):
        block = r.w1[chip // 4, (chip // 2) % 2, chip % 2, :, 4 * D : W1].astype(full)
        for core in range(2):
            first = ((2 * chip + core) * GROUP) // 128 * 128
            r.vecs[0:16, first : first + 256] += block[core * GROUP : core * GROUP + 16]

    def vector(k):
        return r.vecs[k : k + 1, 0:D]

    def w1_cols(k):
        return r.w1[:, :, :, :, k * D : (k + 1) * D].reshape(D, D)

    def wf_cols(k):
        return r.wf[:, :, :, :, k * D : (k + 1) * D].reshape(D, D)

    def wp_rows(k):
        return r.wp[k : k + 1].reshape(FF // depth, D)

    def transpose_half(value):
        return value.astype(full).T.astype(half)

    def share(ref, value):
        ref[:, :, :, :, 0:TOK] = transpose_half(value).reshape(ref.shape[:4] + (TOK,))
        return push(ref.at[:, :, :, :, pl.ds(0, TOK)], ref.at[:, :, :, :, pl.ds(TOK, TOK)], cp)

    first_in = (r.normed[...] * vector(0) + vector(1)).astype(half)

    def qkv_chunk(k):
        value = product(first_in, w1_cols(k))
        if k != 1:
            value = value + vector(2 if k == 0 else 3)
        r.qkv[:, k * D : (k + 1) * D] = value.astype(half)

    qkv_chunk(0)
    gf.side(1)
    gf.near(3)
    qkv_chunk(1)
    gf.side(2)
    qkv_chunk(2)
    gf.deep(1)
    gf.side(3)
    gf.side_done()

    scale = 1.0 / math.sqrt(HD)

    def head_forward(h):
        lo = h * HD
        q, k = r.qkv[:, lo : lo + HD], r.qkv[:, D + lo : D + lo + HD]
        v = r.qkv[:, 2 * D + lo : 2 * D + lo + HD]
        scores = jnp.where(r.allowed[...] > 0.5, product_nt(q, k) * scale, masked_score)
        highest = jnp.max(scores, axis=1, keepdims=True)
        raised = jnp.exp(scores - highest)
        probs = raised / jnp.sum(raised, axis=1, keepdims=True)
        r.probs[h] = probs
        r.mixed[:, lo : lo + HD] = product(probs.astype(half), v).astype(half)

    for h in range(0, 3):
        head_forward(h)
    gf.deep(2)
    for h in range(3, 6):
        head_forward(h)
    gf.deep(3)
    for h in range(6, 9):
        head_forward(h)
    gp.near(1)
    gp.side(0)
    for h in range(9, H):
        head_forward(h)
    gp.near(2)
    gp.side(1)

    residual = tok[...].astype(full) + product(r.mixed[...], w1_cols(3)) + vector(4)
    r.resid[...] = residual
    center = residual - jnp.mean(residual, axis=1, keepdims=True)
    inverse = lax.rsqrt(jnp.mean(center * center, axis=1, keepdims=True) + norm_eps)
    normed = center * inverse
    r.normed2[...] = normed
    r.inverse2[...] = jnp.broadcast_to(inverse, (TOK, 128))
    r.second[...] = (normed * vector(5) + vector(6)).astype(half)
    gf.last()
    gp.near(3)
    gp.side(2)
    share_at = share(r.att, r.mixed[...])
    share_a1 = share(r.a1t, first_in)
    share_a2 = share(r.a2t, r.second[...])
    gf.finish()

    shares = {}

    def hidden_chunk(k):
        cols = pl.ds(k * D, D)
        before = product(r.second[...], wf_cols(k)) + vector(8 + k)
        value_part, slope_part = gelu_parts(before)
        r.slope[:, cols] = slope_part
        act = value_part.astype(half)
        r.hidden[:, cols] = act
        piece = r.hidt.at[pl.ds(k, 1)]
        r.hidt[k : k + 1, :, :, :, 0:TOK] = transpose_half(act).reshape(1, 2, 2, 2 * P_ROWS, TOK)
        shares[k] = push(piece.at[:, :, :, :, pl.ds(0, TOK)], piece.at[:, :, :, :, pl.ds(TOK, TOK)], cp)

    hidden_chunk(0)
    gp.side(3)
    gp.side_done()
    gp.deep(1)
    hidden_chunk(1)
    hidden_chunk(2)
    gp.deep(2)
    hidden_chunk(3)
    gp.deep(3)

    class Scatter:
        def __init__(self, k, dots):
            self.r = part_refs[k]
            self.rows, self.cut, self.width = ROWS_OF[k], FIRST_OF[k], WIDTH_OF[k]
            self.dots = dots

        def multiply(self):
            self.a1, self.b1, self.a2, self.b2, self.a3 = {}, {}, {}, {}, {}
            give_a, give_b = self.r.give_a, self.r.give_b
            keep_a, keep_b = self.r.keep_a, self.r.keep_b
            shape_a = (2, self.rows, self.cut)
            shape_b = (2, self.rows, self.width - self.cut)
            for d in (1, 2, 3, 0):
                u = (z + d) % depth
                give_a[u] = self.dots(0, lambda ref: ref[u, 1 - y]).astype(half).reshape(shape_a)
                self.a1[d] = push(give_a.at[u], self.r.land_a.at[u], yp)
                give_b[u] = self.dots(1, lambda ref: ref[u, :, 1 - x]).astype(half).reshape(shape_b)
                self.b1[d] = push(give_b.at[u], self.r.land_b.at[u], xp)
            for d in (1, 2, 3, 0):
                u = (z + d) % depth
                keep_a[u] = self.dots(0, lambda ref: ref[u, y]).reshape(shape_a)
                keep_b[u] = self.dots(1, lambda ref: ref[u, :, x]).reshape(shape_b)

        def second(self, d):
            u = (z + d) % depth
            self.a1[d].wait_recv()
            keep, land = self.r.keep_a, self.r.land_a
            self.r.sa2[u] = (keep[u, 1 - x] + land[u, 1 - x].astype(full)).astype(half)
            self.a2[d] = push(self.r.sa2.at[u], self.r.ra2.at[u], xp)
            self.b1[d].wait_recv()
            keep, land = self.r.keep_b, self.r.land_b
            if d:
                self.r.sb2[u] = (keep[u] + land[u].astype(full)).astype(half)
                self.b2[d] = push(self.r.sb2.at[u], self.r.rb2.at[d - 1], z_devices[d - 1])
            else:
                keep[u] = keep[u] + land[u].astype(full)

        def third(self, d):
            u = (z + d) % depth
            self.a2[d].wait_recv()
            total = (
                self.r.keep_a[u, x]
                + self.r.land_a[u, x].astype(full)
                + self.r.ra2[u].astype(full)
            )
            if d:
                self.r.sa3[u] = total.astype(half)
                self.a3[d] = push(self.r.sa3.at[u], self.r.ra3.at[d - 1], z_devices[d - 1])
            else:
                self.r.fin[:, 0 : self.cut] = total

        def fourth(self):
            keep = self.r.keep_b
            total = keep[z]
            for d in range(1, depth):
                self.b2[d].wait_recv()
                total += self.r.rb2[d - 1].astype(full)
            keep[z] = total
            self.r.sb3[...] = keep[z, 1 - y].astype(half)
            self.b3 = push(self.r.sb3, self.r.rb3, yp)

        def fifth(self):
            fin = self.r.fin
            total = fin[:, 0 : self.cut]
            for d in range(1, depth):
                self.a3[d].wait_recv()
                total += self.r.ra3[d - 1].astype(full)
            fin[:, 0 : self.cut] = total
            self.b3.wait_recv()
            fin[:, self.cut :] = self.r.keep_b[z, y] + self.r.rb3[...].astype(full)
            size = self.rows // 2
            theirs = pl.ds(pl.multiple_of((1 - c) * size, 8), size)
            self.swap = push(fin.at[theirs, :], self.r.rfin, cp)

        def finish(self, store):
            size = self.rows // 2
            store(c, self.r.fin[pl.ds(pl.multiple_of(c * size, 8), size), :])
            self.swap.wait_recv()
            store(1 - c, self.r.rfin[...])

    def flat(value):
        return value.reshape(-1, 2 * TOK)

    def dots_p(s, pick):
        left = flat(pick(r.hidt))
        return product(left, r.rhsp[:, 256:384] if s else r.rhsp[:, 0:256])

    def dots_f(s, pick):
        left = flat(pick(r.a2t))
        return product(left, r.rhsf[:, 1024:1536] if s else r.rhsf[:, 0:1024])

    def dots_1(s, pick):
        left = flat(pick(r.a1t))
        if s == 0:
            return product(left, r.rhs1[:, 0:1024])
        part = product(left, r.rhs1[:, 1024:1152])
        return jnp.concatenate([part, product(flat(pick(r.att)), r.rhs1[:, 1152:1536])], axis=1)

    cot_copy.wait_recv()
    for k in range(4):
        shares[k].wait_recv()
    sp, sf, s1 = Scatter(0, dots_p), Scatter(1, dots_f), Scatter(2, dots_1)
    sp.multiply()
    gp.last()
    gp.finish()

    vterm = r.vterm
    vterm[...] = jnp.zeros((16, D), full)
    vterm[7:8, :] = jnp.sum(cot[...].astype(full), axis=0, keepdims=True)
    second_grad = jnp.zeros((TOK, D), full)
    for k in range(4):
        cols = pl.ds(k * D, D)
        grad = (product_nt(cot[...], wp_rows(k)) * r.slope[:, cols]).astype(half)
        r.pre[:, cols] = grad
        vterm[8 + k : 9 + k, :] = jnp.sum(grad.astype(full), axis=0, keepdims=True)
    r.rhsf[0:TOK, :] = r.pre[:, lanes(c * F_HALF, F_HALF)]
    pre_copy = push(
        r.pre.at[:, lanes((1 - c) * F_HALF, F_HALF)], r.rhsf.at[pl.ds(TOK, TOK), :], cp
    )
    sp.second(1)
    for k in range(4):
        second_grad += product_nt(r.pre[:, k * D : (k + 1) * D], wf_cols(k))
    pre_copy.wait_recv()
    share_a2.wait_recv()
    sf.multiply()
    sp.second(2)

    def norm_back(upstream, normed, inverse, gain):
        scaled = upstream * gain
        mean_term = jnp.mean(scaled, axis=1, keepdims=True)
        proj_term = jnp.mean(scaled * normed, axis=1, keepdims=True)
        return inverse * (scaled - mean_term - normed * proj_term)

    normed = r.normed2[...]
    vterm[5:6, :] = jnp.sum(second_grad * normed, axis=0, keepdims=True)
    vterm[6:7, :] = jnp.sum(second_grad, axis=0, keepdims=True)
    resid_grad = cot[...].astype(full) + norm_back(
        second_grad, normed, r.inverse2[:, 0:1], vector(5)
    )
    block = r.resid[...] + vector(7)
    r.resid[...] = resid_grad
    resid_half = resid_grad.astype(half)
    r.up[...] = resid_half
    vterm[4:5, :] = jnp.sum(resid_grad, axis=0, keepdims=True)
    r.rhs1[0:TOK, 1152:1536] = r.up[:, lanes(c * 384, 384)]
    one_copies = [
        push(
            r.up.at[:, lanes((1 - c) * 384, 384)],
            r.rhs1.at[pl.ds(TOK, TOK), pl.ds(1152, 384)],
            cp,
        )
    ]
    attended_grad = product_nt(resid_half, w1_cols(3)).astype(half)
    r.mixed[...] = attended_grad

    def head_backward(h):
        lo = h * HD
        q, k = r.qkv[:, lo : lo + HD], r.qkv[:, D + lo : D + lo + HD]
        v = r.qkv[:, 2 * D + lo : 2 * D + lo + HD]
        grad = r.mixed[:, lo : lo + HD]
        probs = r.probs[h]
        value_grad = product_tn(probs.astype(half), grad)
        prob_grad = product_nt(grad, v)
        delta = jnp.sum(probs * prob_grad, axis=1, keepdims=True)
        score_grad = (probs * (prob_grad - delta) * scale).astype(half)
        r.qg[:, lo : lo + HD] = product(score_grad, k).astype(half)
        r.qg[:, D + lo : D + lo + HD] = product_tn(score_grad, q).astype(half)
        r.qg[:, 2 * D + lo : 2 * D + lo + HD] = value_grad.astype(half)

    sp.second(3)
    for h in range(0, 4):
        head_backward(h)
    sp.third(1)
    sp.second(0)
    for h in range(4, 8):
        head_backward(h)
    sp.third(2)
    sp.third(3)
    for h in range(8, H):
        head_backward(h)
    for k in range(3):
        r.rhs1[0:TOK, k * 384 : (k + 1) * 384] = r.qg[:, lanes(k * D + c * 384, 384)]
        one_copies.append(
            push(
                r.qg.at[:, lanes(k * D + (1 - c) * 384, 384)],
                r.rhs1.at[pl.ds(TOK, TOK), pl.ds(k * 384, 384)],
                cp,
            )
        )
    sp.third(0)
    sp.fourth()
    for copy in one_copies + [share_a1, share_at]:
        copy.wait_recv()
    s1.multiply()
    sf.second(1)
    sf.second(2)

    first_grad = jnp.zeros((TOK, D), full)
    for k in range(3):
        first_grad += product_nt(r.qg[:, k * D : (k + 1) * D], w1_cols(k))
    normed = r.normed[...]
    vterm[0:1, :] = jnp.sum(first_grad * normed, axis=0, keepdims=True)
    vterm[1:2, :] = jnp.sum(first_grad, axis=0, keepdims=True)
    vterm[2:3, :] = jnp.sum(r.qg[:, 0:D].astype(full), axis=0, keepdims=True)
    vterm[3:4, :] = jnp.sum(r.qg[:, 2 * D :].astype(full), axis=0, keepdims=True)
    vsend, vrecv = r.vsend, r.vrecv
    vcopy = push(vterm.at[:, lanes((1 - c) * 384, 384)], vrecv.at[0], cp)
    tok_grad = r.resid[...] + norm_back(first_grad, normed, r.inverse[:, 0:1], vector(0))
    tok_out[...] = tok_grad.astype(half)
    sf.third(1)
    vcopy.wait_recv()
    vsend[0] = vterm[:, lanes(c * 384, 384)] + vrecv[0]
    vcopy = push(vsend.at[0], vrecv.at[1], yp)
    sf.second(3)
    sf.third(2)
    sp.fifth()
    for k in range(4):
        block += product(r.hidden[:, k * D : (k + 1) * D], wp_rows(k))
    block_out[...] = block.astype(half)
    sf.second(0)
    sf.third(3)
    vcopy.wait_recv()
    vsend[1] = vsend[0] + vrecv[1]
    vcopy = push(vsend.at[1], vrecv.at[2], xp)
    sf.third(0)
    sf.fourth()
    s1.second(1)
    s1.second(2)
    s1.third(1)
    vcopy.wait_recv()
    vsend[2] = vsend[1] + vrecv[2]
    vlast = [push(vsend.at[2], r.vz.at[d - 1], z_devices[d - 1]) for d in range(1, depth)]
    s1.second(3)
    s1.third(2)

    def store_p(owner, value):
        proj_out[:, lanes(owner * 384, 384)] = value

    def store_f(owner, value):
        wide_out[:, lanes(4 * D + owner * F_HALF, F_HALF)] = value

    def store_1(owner, value):
        for k in range(4):
            wide_out[:, lanes(k * D + owner * 384, 384)] = value[:, k * 384 : (k + 1) * 384]

    sp.finish(store_p)
    sf.fifth()
    s1.second(0)
    s1.third(3)
    s1.fourth()
    s1.third(0)
    total = vsend[2]
    for d in range(depth - 1):
        vlast[d].wait_recv()
        total += r.vz[d]
    vsend[3] = total
    vcopy = push(vsend.at[3], vrecv.at[3], cp)
    vec_out[:, lanes(c * 384, 384)] = total
    sf.finish(store_f)
    s1.fifth()
    vcopy.wait_recv()
    vec_out[:, lanes((1 - c) * 384, 384)] = vrecv[3]
    s1.finish(store_1)
    for copy in sends:
        copy.wait_send()


def block_all(n, tok, lens, cot, wide, proj, vec):
    depth = n // 8
    spaces, parts = scratch_of(depth)
    space = pl.BlockSpec(memory_space=pltpu.VMEM)
    scalars = pl.BlockSpec(memory_space=pltpu.SMEM)
    return pl.pallas_call(
        functools.partial(block_kernel, n, (tuple(spaces), tuple(parts[0]))),
        out_shape=(
            jax.ShapeDtypeStruct((TOK, D), jnp.bfloat16),
            jax.ShapeDtypeStruct((TOK, D), jnp.bfloat16),
            jax.ShapeDtypeStruct((GROUP, 8 * D), jnp.float32),
            jax.ShapeDtypeStruct((P_ROWS, D), jnp.float32),
            jax.ShapeDtypeStruct((16, D), jnp.float32),
        ),
        in_specs=[space, scalars, space, space, space, space],
        out_specs=(space,) * 5,
        scratch_shapes=[pltpu.SemaphoreType.DMA((COPIES,))] * 2
        + list(spaces.values())
        + [space for part in parts for space in part.values()],
        compiler_params=pltpu.CompilerParams(
            collective_id=0, has_side_effects=True, vmem_limit_bytes=58 * 2**20
        ),
    )(tok, lens, cot, wide, proj, vec)


def body_plain(
    tokens,
    seq_lengths,
    cotangent,
    wide_weights,
    proj_weights,
    vector_params,
    wide_moments,
    proj_moments,
    vector_moments,
):
    shards = (
        wide_weights.astype(jnp.bfloat16),
        proj_weights.astype(jnp.bfloat16),
        vector_params.astype(jnp.bfloat16),
    )
    wide_full, proj_full, vector_full = (
        lax.all_gather(shards[0], "fsdp", axis=0, tiled=True),
        lax.all_gather(shards[1], "fsdp", axis=0, tiled=True),
        lax.all_gather(shards[2], "fsdp", axis=1, tiled=True),
    )
    vectors = vector_full.astype(jnp.float32)
    row_count = tokens.shape[0]
    allowed = allowed_pairs(seq_lengths[0], row_count)
    ratio = FF // D
    local_rows = wide_weights.shape[0]
    unscale = math.sqrt(lax.axis_size("fsdp") * row_count)
    gain_one, shift_one, query_bias, value_bias = (vectors[0], vectors[1], vectors[2], vectors[3])
    out_bias, gain_two, shift_two, proj_bias = (vectors[4], vectors[5], vectors[6], vectors[7])
    fc_bias = vectors[8:].reshape(FF)
    token_float = tokens.astype(jnp.float32)
    first_norm, normed_one, inverse_one = norm_forward(token_float, gain_one, shift_one)
    first_in = first_norm.astype(jnp.bfloat16)
    qkv_bias = jnp.concatenate([query_bias, jnp.zeros_like(query_bias), value_bias])
    qkv_half = (
        jnp.dot(first_in, wide_full[:, : 3 * D], preferred_element_type=jnp.float32) + qkv_bias
    ).astype(jnp.bfloat16)
    queries = qkv_half[:, :D]
    key_rows = qkv_half[:, D : 2 * D]
    value_rows = qkv_half[:, 2 * D :]
    attended, logsum = attention_forward(queries, key_rows, value_rows, allowed)
    residual = (
        token_float
        + jnp.dot(attended, wide_full[:, 3 * D : 4 * D], preferred_element_type=jnp.float32)
        + out_bias
    )
    second_norm, normed_two, inverse_two = norm_forward(residual, gain_two, shift_two)
    second_in = second_norm.astype(jnp.bfloat16)
    before_act = (
        jnp.dot(second_in, wide_full[:, 4 * D :], preferred_element_type=jnp.float32) + fc_bias
    )
    value_part, slope_part = gelu_parts(before_act)
    hidden = value_part.astype(jnp.bfloat16)
    block_output = (
        residual + jnp.dot(hidden, proj_full, preferred_element_type=jnp.float32) + proj_bias
    ).astype(jnp.bfloat16)
    backward_wide, backward_proj, vector_again = wide_full, proj_full, vector_full
    backward_vectors = vector_again.astype(jnp.float32)
    qkv_back = backward_wide[:, : 3 * D]
    out_back = backward_wide[:, 3 * D : 4 * D]
    fc_back = backward_wide[:, 4 * D :]
    cot_float = cotangent.astype(jnp.float32)
    proj_bias_grad = jnp.sum(cot_float, axis=0)
    hidden_grad = jnp.einsum(
        "td,fd->tf", cotangent, backward_proj, preferred_element_type=jnp.float32
    )
    pre_grad = (hidden_grad * slope_part).astype(jnp.bfloat16)
    fc_bias_grad = jnp.sum(pre_grad, axis=0, dtype=jnp.float32)
    second_grad = jnp.einsum("tf,df->td", pre_grad, fc_back, preferred_element_type=jnp.float32)
    resid_norm_grad, gain_two_grad, shift_two_grad = norm_backward(
        second_grad, normed_two, inverse_two, backward_vectors[5]
    )
    resid_grad = cot_float + resid_norm_grad
    mlp_vectors = jnp.concatenate(
        [
            jnp.stack([gain_two_grad, shift_two_grad, proj_bias_grad]),
            fc_bias_grad.reshape(ratio, D),
        ],
        axis=0,
    )
    resid_half = resid_grad.astype(jnp.bfloat16)
    out_bias_grad = jnp.sum(resid_grad, axis=0)
    attended_grad = jnp.einsum(
        "te,de->td", resid_half, out_back, preferred_element_type=jnp.float32
    ).astype(jnp.bfloat16)
    qkv_grad = attention_backward(queries, key_rows, value_rows, allowed, logsum, attended_grad)
    query_bias_grad = jnp.sum(qkv_grad[:, :D], axis=0, dtype=jnp.float32)
    value_bias_grad = jnp.sum(qkv_grad[:, 2 * D :], axis=0, dtype=jnp.float32)
    first_grad = jnp.einsum("tc,dc->td", qkv_grad, qkv_back, preferred_element_type=jnp.float32)
    token_norm_grad, gain_one_grad, shift_one_grad = norm_backward(
        first_grad, normed_one, inverse_one, backward_vectors[0]
    )
    tokens_grad = (resid_grad + token_norm_grad).astype(jnp.bfloat16)
    attn_vectors = jnp.stack(
        [gain_one_grad, shift_one_grad, query_bias_grad, value_bias_grad, out_bias_grad]
    )
    vector_terms = jnp.concatenate([attn_vectors, mlp_vectors], axis=0)
    fc_part = column_term(second_in, pre_grad)
    proj_part = column_term(hidden, cotangent).reshape(
        local_rows * lax.axis_size("fsdp"), ratio * D
    )
    qkv_part = column_term(first_in, qkv_grad)
    out_part = column_term(attended, resid_half)
    joined_shard = lax.psum_scatter(
        jnp.concatenate(
            [
                jnp.concatenate([qkv_part, out_part], axis=1),
                jnp.concatenate([fc_part, proj_part], axis=1),
            ],
            axis=1,
        ),
        "fsdp",
        scatter_dimension=0,
        tiled=True,
    )
    wide_grad = joined_shard[:, : 4 * D + FF]
    proj_grad = joined_shard[:, 4 * D + FF :].reshape(local_rows * ratio, D)
    vector_grad = lax.psum_scatter(vector_terms, "fsdp", scatter_dimension=1, tiled=True)
    wide_new, wide_moments_new = adam_update(
        wide_weights, wide_moments, wide_grad, rate_matrix, weight_decay, unscale
    )
    proj_new, proj_moments_new = adam_update(
        proj_weights, proj_moments, proj_grad, rate_matrix, weight_decay, unscale
    )
    vector_new, vector_moments_new = adam_update(
        vector_params, vector_moments, vector_grad, rate_vector, 0.0, unscale
    )
    return (
        block_output,
        tokens_grad,
        wide_grad,
        proj_grad,
        vector_grad,
        wide_new,
        proj_new,
        vector_new,
        wide_moments_new,
        proj_moments_new,
        vector_moments_new,
    )


def body(
    tokens,
    seq_lengths,
    cotangent,
    wide_weights,
    proj_weights,
    vector_params,
    wide_moments,
    proj_moments,
    vector_moments,
):
    n = lax.axis_size("fsdp")
    if not (n == 32 and wide_weights.shape[0] == GROUP and tokens.shape[0] == TOK):
        return body_plain(
            tokens,
            seq_lengths,
            cotangent,
            wide_weights,
            proj_weights,
            vector_params,
            wide_moments,
            proj_moments,
            vector_moments,
        )
    me = lax.axis_index("fsdp")
    rows, columns = vector_params.shape
    block_output, tokens_grad, wide_grad, proj_grad, vector_sum = block_all(
        n, tokens, seq_lengths, cotangent, wide_weights, proj_weights, vector_params
    )
    vector_grad = lax.dynamic_slice(vector_sum, (0, me * columns), (rows, columns))
    unscale = math.sqrt(n * tokens.shape[0])
    wide_new, wide_moments_new = adam_update(
        wide_weights, wide_moments, wide_grad, rate_matrix, weight_decay, unscale
    )
    proj_new, proj_moments_new = adam_update(
        proj_weights, proj_moments, proj_grad, rate_matrix, weight_decay, unscale
    )
    vector_new, vector_moments_new = adam_update(
        vector_params, vector_moments, vector_grad, rate_vector, 0.0, unscale
    )
    return (
        block_output,
        tokens_grad,
        wide_grad,
        proj_grad,
        vector_grad,
        wide_new,
        proj_new,
        vector_new,
        wide_moments_new,
        proj_moments_new,
        vector_moments_new,
    )


def solution(mesh):
    placed = (
        P("fsdp", None),
        P("fsdp", None),
        P("fsdp", None),
        P("fsdp", None),
        P("fsdp", None),
        P(None, "fsdp"),
        P(None, "fsdp", None),
        P(None, "fsdp", None),
        P(None, None, "fsdp"),
    )
    return jax.shard_map(
        body,
        mesh=mesh,
        in_specs=placed,
        out_specs=(
            P("fsdp", None),
            P("fsdp", None),
            P("fsdp", None),
            P("fsdp", None),
            P(None, "fsdp"),
            P("fsdp", None),
            P("fsdp", None),
            P(None, "fsdp"),
            P(None, "fsdp", None),
            P(None, "fsdp", None),
            P(None, None, "fsdp"),
        ),
        check_vma=False,
    )
```

```python
import functools
import math
import types

import jax
import jax.numpy as jnp
from jax import lax
from jax.experimental import pallas as pl
from jax.experimental.pallas import tpu as pltpu
from jax.sharding import PartitionSpec as P

D = 768
H = 12
HD = 64
FF = 3072
STEP = 2


norm_eps = 1e-05
beta_one = 0.9
beta_two = 0.95
adam_eps = 1e-08
rate_matrix = 0.02
rate_vector = 0.2
weight_decay = 0.1
gelu_coeff = 0.7978845608028654
masked_score = -1e30


def norm_forward(values, gain_row, offset):
    center = values - jnp.mean(values, axis=1, keepdims=True)
    variance = jnp.mean(center * center, axis=1, keepdims=True)
    inverse = lax.rsqrt(variance + norm_eps)
    normed = center * inverse
    return (normed * gain_row + offset, normed, inverse)


def norm_backward(upstream, normed, inverse, gain_row):
    scaled = upstream * gain_row
    mean_term = jnp.mean(scaled, axis=1, keepdims=True)
    proj_term = jnp.mean(scaled * normed, axis=1, keepdims=True)
    input_grad = inverse * (scaled - mean_term - normed * proj_term)
    return (input_grad, jnp.sum(upstream * normed, axis=0), jnp.sum(upstream, axis=0))


def gelu_parts(before):
    inner_arg = gelu_coeff * (before + 0.044715 * before * before * before)
    tangent = jnp.tanh(inner_arg)
    value_part = 0.5 * before * (1.0 + tangent)
    slope_part = 0.5 * (1.0 + tangent) + 0.5 * before * (1.0 - tangent * tangent) * gelu_coeff * (
        1.0 + 3.0 * 0.044715 * before * before
    )
    return (value_part, slope_part)


def allowed_pairs(length_row, row_count):
    order = jnp.arange(length_row.shape[0], dtype=jnp.int32)
    bounds = jnp.sum(jnp.where(order[None, :] <= order[:, None], length_row[None, :], 0), axis=1)
    position = jnp.arange(row_count, dtype=jnp.int32)
    segment = jnp.sum((position[:, None] >= bounds[None, :]).astype(jnp.int32), axis=1)
    return (segment[:, None] == segment[None, :]) & (position[None, :] <= position[:, None])


def head_view(matrix):
    return matrix.reshape(matrix.shape[0], H, HD)


def score_table(queries, key_rows, allowed):
    scale_factor = 1.0 / math.sqrt(HD)
    scores = (
        jnp.einsum(
            "qhd,khd->hqk",
            head_view(queries),
            head_view(key_rows),
            preferred_element_type=jnp.float32,
        )
        * scale_factor
    )
    return jnp.where(allowed[None, :, :], scores, masked_score)


def attention_forward(queries, key_rows, value_rows, allowed):
    scores = score_table(queries, key_rows, allowed)
    highest = jnp.max(scores, axis=2, keepdims=True)
    logsum = highest + jnp.log(jnp.sum(jnp.exp(scores - highest), axis=2, keepdims=True))
    weights = jnp.exp(scores - logsum).astype(jnp.bfloat16)
    mixed = jnp.einsum(
        "hqk,khd->qhd", weights, head_view(value_rows), preferred_element_type=jnp.float32
    )
    return (mixed.reshape(queries.shape[0], D).astype(jnp.bfloat16), logsum)


def attention_backward(queries, key_rows, value_rows, allowed, logsum, upstream):
    scale_factor = 1.0 / math.sqrt(HD)
    scores = score_table(queries, key_rows, allowed)
    probs = jnp.exp(scores - logsum)
    rounded = probs.astype(jnp.bfloat16)
    grad_heads = head_view(upstream)
    value_grad = jnp.einsum("hqk,qhd->khd", rounded, grad_heads, preferred_element_type=jnp.float32)
    prob_grad = jnp.einsum(
        "qhd,khd->hqk", grad_heads, head_view(value_rows), preferred_element_type=jnp.float32
    )
    delta_row = jnp.sum(probs * prob_grad, axis=2, keepdims=True)
    score_grad = (probs * (prob_grad - delta_row) * scale_factor).astype(jnp.bfloat16)
    query_grad = jnp.einsum(
        "hqk,khd->qhd", score_grad, head_view(key_rows), preferred_element_type=jnp.float32
    )
    key_grad = jnp.einsum(
        "hqk,qhd->khd", score_grad, head_view(queries), preferred_element_type=jnp.float32
    )
    row_total = queries.shape[0]
    joined = jnp.concatenate(
        [
            query_grad.reshape(row_total, D),
            key_grad.reshape(row_total, D),
            value_grad.reshape(row_total, D),
        ],
        axis=1,
    )
    return joined.astype(jnp.bfloat16)


def adam_update(weights, moments, gradient, rate, decay_rate, unscale):
    scaled_grad = gradient / unscale
    first_moment = beta_one * moments[0] + (1.0 - beta_one) * scaled_grad
    second_moment = beta_two * moments[1] + (1.0 - beta_two) * scaled_grad * scaled_grad
    corrected_first = first_moment / (1.0 - beta_one**STEP)
    corrected_second = second_moment / (1.0 - beta_two**STEP)
    updated = weights - rate * (
        corrected_first / (jnp.sqrt(corrected_second) + adam_eps) + decay_rate * weights
    )
    return (updated, jnp.stack([first_moment, second_moment]))


def column_term(left, right):
    return jnp.einsum("tc,te->ce", left, right, preferred_element_type=jnp.float32)


MESH = pl.DeviceIdType.MESH
GROUP = 24


def position(n):
    depth = n // 8
    me = lax.axis_index("fsdp")
    return depth, me // 8, (me // 4) % 2, (me // 2) % 2, me % 2


def device_at(z, y, x, c):
    return ((z * 2 + y) * 2 + x) * 2 + c


def greet(partners):
    barrier = pltpu.get_barrier_semaphore()
    for device in partners:
        pl.semaphore_signal(barrier, inc=1, device_id=(device,), device_id_type=MESH)
    pl.semaphore_wait(barrier, len(partners))


def remote(src, dst, send, recv, device):
    return pltpu.make_async_remote_copy(
        src_ref=src,
        dst_ref=dst,
        send_sem=send,
        recv_sem=recv,
        device_id=(device,),
        device_id_type=MESH,
    )


def product(left, right):
    return jnp.dot(left, right, preferred_element_type=jnp.float32)


def product_nt(left, right):
    return lax.dot_general(
        left, right, (((1,), (1,)), ((), ())), preferred_element_type=jnp.float32
    )


def product_tn(left, right):
    return lax.dot_general(
        left, right, (((0,), (0,)), ((), ())), preferred_element_type=jnp.float32
    )


TOK = 128
UNIT = 2 * GROUP
W1 = 4 * D + 256
W1_HALF = W1 // 2
W1_FIRST = 1024
F_HALF = FF // 2
F_FIRST = 1024
P_ROWS = FF // 32
P_FIRST = 64
ROWS_OF = (2 * P_ROWS, UNIT, UNIT)
FIRST_OF = (256, 1024, 896)
WIDTH_OF = (384, 1536, 1536)


def scratch_of(depth):
    half, full = jnp.bfloat16, jnp.float32

    def vmem(shape, dtype):
        return pltpu.VMEM(shape, dtype)

    lead = (depth, 2, 2)
    spaces = dict(
        ext=vmem((32, 4 * D + 256 + FF), half),
        ext_in=vmem((32, 4 * D + 256 + FF), half),
        w1=vmem(lead + (UNIT, W1), half),
        wf=vmem(lead + (UNIT, FF), half),
        wp=vmem(lead + (2 * P_ROWS, D), half),
        vecs=vmem((16, D + 128), full),
        normed=vmem((TOK, D), full),
        inverse=vmem((TOK, 128), full),
        normed2=vmem((TOK, D), full),
        inverse2=vmem((TOK, 128), full),
        allowed=vmem((TOK, TOK), full),
        window=vmem((GROUP, 256), full),
        qkv=vmem((TOK, 3 * D), half),
        probs=vmem((H, TOK, TOK), full),
        mixed=vmem((TOK, D), half),
        resid=vmem((TOK, D), full),
        second=vmem((TOK, D), half),
        slope=vmem((TOK, FF), full),
        hidden=vmem((TOK, FF), half),
        pre=vmem((TOK, FF), half),
        up=vmem((TOK, D), half),
        qg=vmem((TOK, 3 * D), half),
        a1t=vmem(lead + (UNIT, 2 * TOK), half),
        att=vmem(lead + (UNIT, 2 * TOK), half),
        a2t=vmem(lead + (UNIT, 2 * TOK), half),
        hidt=vmem(lead + (2 * P_ROWS, 2 * TOK), half),
        rhsp=vmem((2 * TOK, 384), half),
        rhsf=vmem((2 * TOK, F_HALF), half),
        rhs1=vmem((2 * TOK, 4 * 384), half),
        vterm=vmem((16, D), full),
        vfull=vmem((16, D), full),
        vsend=vmem((4, 16, 384), full),
        vrecv=vmem((4, 16, 384), full),
        vz=vmem((depth - 1, 16, 384), full),
    )
    parts = []
    for k in range(3):
        rows, first, width = ROWS_OF[k], FIRST_OF[k], WIDTH_OF[k]
        rest = width - first
        parts.append(
            dict(
                give_a=vmem((depth, 2, rows, first), half),
                land_a=vmem((depth, 2, rows, first), half),
                keep_a=vmem((depth, 2, rows, first), full),
                give_b=vmem((depth, 2, rows, rest), half),
                land_b=vmem((depth, 2, rows, rest), half),
                keep_b=vmem((depth, 2, rows, rest), full),
                sa2=vmem((depth, rows, first), half),
                ra2=vmem((depth, rows, first), half),
                sa3=vmem((depth, rows, first), half),
                ra3=vmem((depth - 1, rows, first), half),
                sb2=vmem((depth, 2, rows, rest), half),
                rb2=vmem((depth - 1, 2, rows, rest), half),
                sb3=vmem((rows, rest), half),
                rb3=vmem((rows, rest), half),
                fin=vmem((rows, width), full),
                rfin=vmem((rows // 2, width), full),
            )
        )
    return spaces, parts


COPIES = 232


def block_kernel(n, names, tok, lens, cot, wide, proj, vec, block_out, tok_out, wide_out, proj_out, vec_out, *refs):
    names, part_names = names
    ssem, rsem = refs[0], refs[1]
    r = types.SimpleNamespace(**dict(zip(names, refs[2:])))
    part_refs = []
    for k in range(3):
        first = 2 + len(names) + k * len(part_names)
        part_refs.append(types.SimpleNamespace(**dict(zip(part_names, refs[first:]))))
    depth, z, y, x, c = position(n)
    z_pair, z_far = z + 1 - 2 * (z % 2), depth - 1 - z
    z_units = (z, z_pair, z_far, depth - 1 - z_pair)
    zp, zq = device_at(z_pair, y, x, c), device_at(z_far, y, x, c)
    yp, xp = device_at(z, 1 - y, x, c), device_at(z, y, 1 - x, c)
    cp = device_at(z, y, x, 1 - c)
    half, full = jnp.bfloat16, jnp.float32
    sends = []
    count = [0]

    def push(src, dst, device, landed=None):
        k = count[0]
        count[0] = k + 1
        copy = remote(src, dst, ssem.at[k], rsem.at[k], device)
        copy.start()
        sends.append(copy)
        landed = dst if landed is None else landed
        return remote(landed, landed, ssem.at[k], rsem.at[k], device)

    def lanes(start, size):
        return pl.ds(pl.multiple_of(start, 128), size)

    wide_now = wide[...].astype(half).astype(full)
    r.window[...] = jnp.zeros((GROUP, 256), full)
    r.window[0 : vec.shape[0], 0 : vec.shape[1]] = vec[...]
    shift = lax.rem(lax.axis_index("fsdp") * vec.shape[1], 128)
    vec_now = pltpu.roll(r.window[...], shift, 1)
    r.ext[0:GROUP, 0 : 4 * D] = wide_now[:, 0 : 4 * D].astype(half)
    r.ext[0:GROUP, 4 * D : W1] = vec_now.astype(half)
    r.ext[0:GROUP, W1:] = wide_now[:, 4 * D :].astype(half)
    r.ext[GROUP:, :] = jnp.zeros((32 - GROUP, W1 + FF), half)
    r.wp[z, y, x, pl.ds(pl.multiple_of(c * P_ROWS, 32), P_ROWS), :] = proj[...].astype(half)
    greet([zp, zq, yp, xp, cp])
    ext_copy = push(r.ext, r.ext_in, cp)

    def w1_at(s):
        start = c * W1_HALF + (W1_FIRST if s else 0)
        size = W1_HALF - W1_FIRST if s else W1_FIRST
        return lambda zi, yi, xi: r.w1.at[zi, yi, xi, :, lanes(start, size)]

    def wf_at(s):
        start = c * F_HALF + (F_FIRST if s else 0)
        size = F_HALF - F_FIRST if s else F_FIRST
        return lambda zi, yi, xi: r.wf.at[zi, yi, xi, :, lanes(start, size)]

    def wp_at(s):
        start = c * P_ROWS + (P_FIRST if s else 0)
        size = P_ROWS - P_FIRST if s else P_FIRST
        return lambda zi, yi, xi: r.wp.at[zi, yi, xi, pl.ds(pl.multiple_of(start, 32), size), :]

    every, both = pl.ds(0, depth), pl.ds(0, 2)

    def zat(d):
        return z_units[d]

    class Gather:
        def __init__(self, a, b, own):
            self.a, self.b, self.own = a, b, own
            self.cores = []

        def core(self, ref, landed):
            self.cores.append((ref, landed))

        def start(self):
            a, b = self.a, self.b
            mine_a, mine_b = a(z, y, x), b(z, y, x)
            self.by = push(mine_b, mine_b, yp, b(z, 1 - y, x))
            self.az, self.bz, self.ax, self.ay, self.bx = {}, {}, {}, {}, {}
            self.ax[0] = push(mine_a, mine_a, xp, a(z, y, 1 - x))
            self.ay[0, 0] = push(mine_a, mine_a, yp, a(z, 1 - y, x))
            self.bx[0, 0] = push(mine_b, mine_b, xp, b(z, y, 1 - x))
            self.done = []
            if self.own:
                self.done.append(push(mine_a, mine_a, cp, OWN_A(z, y, x)))
                self.done.append(push(mine_b, mine_b, cp, OWN_B(z, y, x)))

        def start_z(self):
            a, b = self.a, self.b
            mine_a, mine_b = a(z, y, x), b(z, y, x)
            for d, device in ((2, zq), (1, zp)):
                self.az[d] = push(mine_a, mine_a, device, a(zat(d), y, x))
            for d, device in ((2, zq), (1, zp)):
                self.bz[d, 0] = push(mine_b, mine_b, device, b(zat(d), y, x))

        def first(self):
            b = self.b
            self.by.wait_recv()
            got = b(z, 1 - y, x)
            for d, device in ((2, zq), (1, zp)):
                self.bz[d, 1] = push(got, got, device, b(zat(d), 1 - y, x))
            self.bx[0, 1] = push(got, got, xp, b(z, 1 - y, 1 - x))
            self.give(b, (z, 1 - y, x))

        def give(self, at, where):
            ref = at(*where)
            self.done.append(push(ref, ref, cp, (PEER_A if at is self.a else PEER_B)[id(self)](*where)))

        def near(self, d):
            a = self.a
            self.az[d].wait_recv()
            got = a(zat(d), y, x)
            if d == 2:
                self.az[3] = push(got, got, zp, a(zat(3), y, x))
            self.ax[d] = push(got, got, xp, a(zat(d), y, 1 - x))
            self.ay[0, d] = push(got, got, yp, a(zat(d), 1 - y, x))
            self.give(a, (zat(d), y, x))

        def side(self, d):
            a = self.a
            self.ax[d].wait_recv()
            got = a(zat(d), y, 1 - x)
            self.ay[1, d] = push(got, got, yp, a(zat(d), 1 - y, 1 - x))

        def side_done(self):
            self.give(self.a, (every, y, 1 - x))

        def deep(self, d):
            b = self.b
            for k, yi in ((0, y), (1, 1 - y)):
                self.bz[d, k].wait_recv()
                got = b(zat(d), yi, x)
                if d == 2:
                    self.bz[3, k] = push(got, got, zp, b(zat(3), yi, x))
                self.bx[d, k] = push(got, got, xp, b(zat(d), yi, 1 - x))
            self.give(b, (zat(d), both, x))

        def last(self):
            for d in (0, 2, 1, 3):
                self.bx[d, 0].wait_recv()
                self.bx[d, 1].wait_recv()
                self.give(self.b, (zat(d), both, 1 - x))
            for d in (0, 2, 1, 3):
                self.ay[0, d].wait_recv()
                self.ay[1, d].wait_recv()
                self.give(self.a, (zat(d), 1 - y, both))

        def finish(self):
            for copy in self.done:
                copy.wait_recv()

    PEER_A, PEER_B = {}, {}

    def peer_at(ref, cut, start_of, size):
        start = start_of(1 - c)
        if cut == "lanes":
            return lambda zi, yi, xi: ref.at[zi, yi, xi, :, lanes(start, size)]
        return lambda zi, yi, xi: ref.at[zi, yi, xi, pl.ds(pl.multiple_of(start, 32), size), :]

    g1 = Gather(w1_at(0), w1_at(1), False)
    gf = Gather(wf_at(0), wf_at(1), False)
    gp = Gather(wp_at(0), wp_at(1), True)
    for g, ref, cut, whole, cut_at in (
        (g1, r.w1, "lanes", W1_HALF, W1_FIRST),
        (gf, r.wf, "lanes", F_HALF, F_FIRST),
        (gp, r.wp, "rows", P_ROWS, P_FIRST),
    ):
        PEER_A[id(g)] = peer_at(ref, cut, lambda k, w=whole: k * w, cut_at)
        PEER_B[id(g)] = peer_at(ref, cut, lambda k, w=whole, o=cut_at: k * w + o, whole - cut_at)
    OWN_A, OWN_B = PEER_A[id(gp)], PEER_B[id(gp)]

    token_float = tok[...].astype(full)
    center = token_float - jnp.mean(token_float, axis=1, keepdims=True)
    inverse = lax.rsqrt(jnp.mean(center * center, axis=1, keepdims=True) + norm_eps)
    r.normed[...] = center * inverse
    r.inverse[...] = jnp.broadcast_to(inverse, (TOK, 128))
    across = lax.broadcasted_iota(jnp.int32, (TOK, TOK), 1)
    down = lax.broadcasted_iota(jnp.int32, (TOK, TOK), 0)
    seg_across = jnp.zeros((TOK, TOK), jnp.int32)
    seg_down = jnp.zeros((TOK, TOK), jnp.int32)
    bound = 0
    for j in range(lens.shape[1]):
        bound = bound + lens[0, j]
        seg_across += (across >= bound).astype(jnp.int32)
        seg_down += (down >= bound).astype(jnp.int32)
    r.allowed[...] = ((seg_across == seg_down) & (across <= down)).astype(full)

    ext_copy.wait_recv()

    def assemble(target, start, size):
        for o in range(0, size, 512):
            w = min(512, size - o)
            mine = r.ext[:, start + o : start + o + w].astype(full)[:GROUP]
            theirs = r.ext_in[:, start + o : start + o + w].astype(full)[:GROUP]
            low = jnp.where(c == 0, mine, theirs)
            high = jnp.where(c == 0, theirs, mine)
            target[z, y, x, :, o : o + w] = jnp.concatenate([low, high], axis=0).astype(half)

    assemble(r.w1, 0, W1)
    g1.start()
    g1.start_z()
    assemble(r.wf, W1, FF)
    gf.start()
    gp.start()
    cot_copy = push(cot.at[:, lanes((1 - c) * 384, 384)], r.rhsp.at[pl.ds(TOK, TOK), :], cp)
    r.rhsp[0:TOK, :] = cot[:, lanes(c * 384, 384)]
    g1.first()
    g1.near(2)
    gf.start_z()
    gf.first()
    g1.side(0)
    g1.near(1)
    g1.side(2)
    g1.deep(2)
    g1.near(3)
    g1.side(1)
    g1.side(3)
    g1.side_done()
    g1.deep(1)
    g1.deep(3)
    gf.near(2)
    gp.start_z()
    gp.first()
    gf.side(0)
    g1.last()
    gf.near(1)
    g1.finish()

    r.vecs[...] = jnp.zeros((16, D + 128), full)
    for chip in range(n // 2):
        block = r.w1[chip // 4, (chip // 2) % 2, chip % 2, :, 4 * D : W1].astype(full)
        for core in range(2):
            first = ((2 * chip + core) * GROUP) // 128 * 128
            r.vecs[0:16, first : first + 256] += block[core * GROUP : core * GROUP + 16]

    def vector(k):
        return r.vecs[k : k + 1, 0:D]

    def w1_cols(k):
        return r.w1[:, :, :, :, k * D : (k + 1) * D].reshape(D, D)

    def wf_cols(k):
        return r.wf[:, :, :, :, k * D : (k + 1) * D].reshape(D, D)

    def wp_rows(k):
        return r.wp[k : k + 1].reshape(FF // depth, D)

    def transpose_half(value):
        return value.astype(full).T.astype(half)

    def share(ref, value):
        ref[:, :, :, :, 0:TOK] = transpose_half(value).reshape(ref.shape[:4] + (TOK,))
        return push(ref.at[:, :, :, :, pl.ds(0, TOK)], ref.at[:, :, :, :, pl.ds(TOK, TOK)], cp)

    first_in = (r.normed[...] * vector(0) + vector(1)).astype(half)

    def qkv_chunk(k):
        value = product(first_in, w1_cols(k))
        if k != 1:
            value = value + vector(2 if k == 0 else 3)
        r.qkv[:, k * D : (k + 1) * D] = value.astype(half)

    qkv_chunk(0)
    gf.side(2)
    gf.near(3)
    qkv_chunk(1)
    gf.side(1)
    qkv_chunk(2)
    gf.deep(2)
    gf.side(3)
    gf.side_done()

    scale = 1.0 / math.sqrt(HD)

    def head_forward(h):
        lo = h * HD
        q, k = r.qkv[:, lo : lo + HD], r.qkv[:, D + lo : D + lo + HD]
        v = r.qkv[:, 2 * D + lo : 2 * D + lo + HD]
        scores = jnp.where(r.allowed[...] > 0.5, product_nt(q, k) * scale, masked_score)
        highest = jnp.max(scores, axis=1, keepdims=True)
        raised = jnp.exp(scores - highest)
        probs = raised / jnp.sum(raised, axis=1, keepdims=True)
        r.probs[h] = probs
        r.mixed[:, lo : lo + HD] = product(probs.astype(half), v).astype(half)

    for h in range(0, 3):
        head_forward(h)
    gf.deep(1)
    for h in range(3, 6):
        head_forward(h)
    gf.deep(3)
    for h in range(6, 9):
        head_forward(h)
    gp.near(2)
    gp.side(0)
    for h in range(9, H):
        head_forward(h)
    gp.near(1)
    gp.side(2)

    residual = tok[...].astype(full) + product(r.mixed[...], w1_cols(3)) + vector(4)
    r.resid[...] = residual
    center = residual - jnp.mean(residual, axis=1, keepdims=True)
    inverse = lax.rsqrt(jnp.mean(center * center, axis=1, keepdims=True) + norm_eps)
    normed = center * inverse
    r.normed2[...] = normed
    r.inverse2[...] = jnp.broadcast_to(inverse, (TOK, 128))
    r.second[...] = (normed * vector(5) + vector(6)).astype(half)
    gf.last()
    gp.near(3)
    gp.side(1)
    share_at = share(r.att, r.mixed[...])
    share_a1 = share(r.a1t, first_in)
    share_a2 = share(r.a2t, r.second[...])
    gf.finish()

    shares = {}

    def hidden_chunk(k):
        cols = pl.ds(k * D, D)
        before = product(r.second[...], wf_cols(k)) + vector(8 + k)
        value_part, slope_part = gelu_parts(before)
        r.slope[:, cols] = slope_part
        act = value_part.astype(half)
        r.hidden[:, cols] = act
        piece = r.hidt.at[pl.ds(k, 1)]
        r.hidt[k : k + 1, :, :, :, 0:TOK] = transpose_half(act).reshape(1, 2, 2, 2 * P_ROWS, TOK)
        shares[k] = push(piece.at[:, :, :, :, pl.ds(0, TOK)], piece.at[:, :, :, :, pl.ds(TOK, TOK)], cp)

    hidden_chunk(0)
    gp.side(3)
    gp.side_done()
    gp.deep(2)
    hidden_chunk(1)
    hidden_chunk(2)
    gp.deep(1)
    hidden_chunk(3)

    class Scatter:
        def __init__(self, k, dots):
            self.r = part_refs[k]
            self.rows, self.cut, self.width = ROWS_OF[k], FIRST_OF[k], WIDTH_OF[k]
            self.dots = dots
            self.a1, self.b1, self.a2, self.b2, self.a3 = {}, {}, {}, {}, {}

        def give_y(self):
            give = self.r.give_a
            for d in (3, 1, 2, 0):
                u = z_units[d]
                value = self.dots(0, lambda ref: ref[u, 1 - y]).astype(half)
                give[u] = value.reshape(2, self.rows, self.cut)
                self.a1[d, 1] = push(give.at[u, 1 - x], self.r.land_a.at[u, 1 - x], yp)
            for d in (3, 1, 2, 0):
                u = z_units[d]
                self.a1[d, 0] = push(give.at[u, x], self.r.land_a.at[u, x], yp)

        def give_x(self):
            give = self.r.give_b
            for d in (3, 1, 2, 0):
                u = z_units[d]
                value = self.dots(1, lambda ref: ref[u, :, 1 - x]).astype(half)
                give[u] = value.reshape(2, self.rows, self.width - self.cut)
                self.b1[d] = push(give.at[u], self.r.land_b.at[u], xp)

        def keep(self):
            for d in (3, 1, 2, 0):
                u = z_units[d]
                value = self.dots(0, lambda ref: ref[u, y])
                self.r.keep_a[u] = value.reshape(2, self.rows, self.cut)
                value = self.dots(1, lambda ref: ref[u, :, x])
                self.r.keep_b[u] = value.reshape(2, self.rows, self.width - self.cut)

        def multiply(self):
            self.give_y()
            self.give_x()
            self.keep()

        def second(self, d):
            u = z_units[d]
            self.a1[d, 1].wait_recv()
            keep, land = self.r.keep_a, self.r.land_a
            self.r.sa2[u] = (keep[u, 1 - x] + land[u, 1 - x].astype(full)).astype(half)
            self.a2[d] = push(self.r.sa2.at[u], self.r.ra2.at[u], xp)
            self.b1[d].wait_recv()
            keep, land = self.r.keep_b, self.r.land_b
            total = keep[u] + land[u].astype(full)
            if d == 2:
                self.b2[3].wait_recv()
                total += self.r.rb2[2].astype(full)
            if d:
                self.r.sb2[u] = total.astype(half)
                self.b2[d] = push(self.r.sb2.at[u], self.r.rb2.at[d - 1], zq if d == 2 else zp)
            else:
                keep[u] = total

        def third(self, d):
            u = z_units[d]
            self.a2[d].wait_recv()
            self.a1[d, 0].wait_recv()
            total = (
                self.r.keep_a[u, x]
                + self.r.land_a[u, x].astype(full)
                + self.r.ra2[u].astype(full)
            )
            if d == 2:
                self.a3[3].wait_recv()
                total += self.r.ra3[2].astype(full)
            if d:
                self.r.sa3[u] = total.astype(half)
                self.a3[d] = push(self.r.sa3.at[u], self.r.ra3.at[d - 1], zq if d == 2 else zp)
            else:
                self.r.fin[:, 0 : self.cut] = total

        def fourth(self):
            keep = self.r.keep_b
            total = keep[z]
            for d in (1, 2):
                self.b2[d].wait_recv()
                total += self.r.rb2[d - 1].astype(full)
            keep[z] = total
            self.r.sb3[...] = keep[z, 1 - y].astype(half)
            self.b3 = push(self.r.sb3, self.r.rb3, yp)

        def fifth(self):
            fin = self.r.fin
            total = fin[:, 0 : self.cut]
            for d in (1, 2):
                self.a3[d].wait_recv()
                total += self.r.ra3[d - 1].astype(full)
            fin[:, 0 : self.cut] = total
            self.b3.wait_recv()
            fin[:, self.cut :] = self.r.keep_b[z, y] + self.r.rb3[...].astype(full)
            size = self.rows // 2
            theirs = pl.ds(pl.multiple_of((1 - c) * size, 8), size)
            self.swap = push(fin.at[theirs, :], self.r.rfin, cp)

        def finish(self, store):
            size = self.rows // 2
            store(c, self.r.fin[pl.ds(pl.multiple_of(c * size, 8), size), :])
            self.swap.wait_recv()
            store(1 - c, self.r.rfin[...])

    def flat(value):
        return value.reshape(-1, 2 * TOK)

    def dots_p(s, pick):
        left = flat(pick(r.hidt))
        return product(left, r.rhsp[:, 256:384] if s else r.rhsp[:, 0:256])

    def dots_f(s, pick):
        left = flat(pick(r.a2t))
        return product(left, r.rhsf[:, 1024:1536] if s else r.rhsf[:, 0:1024])

    def dots_1(s, pick):
        left = flat(pick(r.a1t))
        if s == 0:
            return product(left, r.rhs1[:, 0:896])
        part = product(left, r.rhs1[:, 896:1152])
        return jnp.concatenate([part, product(flat(pick(r.att)), r.rhs1[:, 1152:1536])], axis=1)

    cot_copy.wait_recv()
    for k in range(4):
        shares[k].wait_recv()
    sp, sf, s1 = Scatter(0, dots_p), Scatter(1, dots_f), Scatter(2, dots_1)
    gp.deep(3)
    sp.multiply()
    gp.last()
    gp.finish()

    vterm = r.vterm
    vterm[...] = jnp.zeros((16, D), full)
    vterm[7:8, :] = jnp.sum(cot[...].astype(full), axis=0, keepdims=True)
    second_grad = jnp.zeros((TOK, D), full)
    for k in range(4):
        cols = pl.ds(k * D, D)
        grad = (product_nt(cot[...], wp_rows(k)) * r.slope[:, cols]).astype(half)
        r.pre[:, cols] = grad
        vterm[8 + k : 9 + k, :] = jnp.sum(grad.astype(full), axis=0, keepdims=True)
    r.rhsf[0:TOK, :] = r.pre[:, lanes(c * F_HALF, F_HALF)]
    pre_copy = push(
        r.pre.at[:, lanes((1 - c) * F_HALF, F_HALF)], r.rhsf.at[pl.ds(TOK, TOK), :], cp
    )
    sp.second(3)
    sp.second(1)
    pre_copy.wait_recv()
    share_a2.wait_recv()
    sf.multiply()
    for k in range(4):
        second_grad += product_nt(r.pre[:, k * D : (k + 1) * D], wf_cols(k))

    def norm_back(upstream, normed, inverse, gain):
        scaled = upstream * gain
        mean_term = jnp.mean(scaled, axis=1, keepdims=True)
        proj_term = jnp.mean(scaled * normed, axis=1, keepdims=True)
        return inverse * (scaled - mean_term - normed * proj_term)

    normed = r.normed2[...]
    vterm[5:6, :] = jnp.sum(second_grad * normed, axis=0, keepdims=True)
    vterm[6:7, :] = jnp.sum(second_grad, axis=0, keepdims=True)
    resid_grad = cot[...].astype(full) + norm_back(
        second_grad, normed, r.inverse2[:, 0:1], vector(5)
    )
    block = r.resid[...] + vector(7)
    r.resid[...] = resid_grad
    resid_half = resid_grad.astype(half)
    r.up[...] = resid_half
    vterm[4:5, :] = jnp.sum(resid_grad, axis=0, keepdims=True)
    r.rhs1[0:TOK, 1152:1536] = r.up[:, lanes(c * 384, 384)]
    one_copies = [
        push(
            r.up.at[:, lanes((1 - c) * 384, 384)],
            r.rhs1.at[pl.ds(TOK, TOK), pl.ds(1152, 384)],
            cp,
        )
    ]
    attended_grad = product_nt(resid_half, w1_cols(3)).astype(half)
    r.mixed[...] = attended_grad

    def head_backward(h):
        lo = h * HD
        q, k = r.qkv[:, lo : lo + HD], r.qkv[:, D + lo : D + lo + HD]
        v = r.qkv[:, 2 * D + lo : 2 * D + lo + HD]
        grad = r.mixed[:, lo : lo + HD]
        probs = r.probs[h]
        value_grad = product_tn(probs.astype(half), grad)
        prob_grad = product_nt(grad, v)
        delta = jnp.sum(probs * prob_grad, axis=1, keepdims=True)
        score_grad = (probs * (prob_grad - delta) * scale).astype(half)
        r.qg[:, lo : lo + HD] = product(score_grad, k).astype(half)
        r.qg[:, D + lo : D + lo + HD] = product_tn(score_grad, q).astype(half)
        r.qg[:, 2 * D + lo : 2 * D + lo + HD] = value_grad.astype(half)

    sp.second(2)
    for h in range(0, 4):
        head_backward(h)
    sp.third(3)
    sp.second(0)
    for h in range(4, 8):
        head_backward(h)
    sp.third(1)
    sp.third(2)
    for h in range(8, H):
        head_backward(h)
    for k in range(3):
        r.rhs1[0:TOK, k * 384 : (k + 1) * 384] = r.qg[:, lanes(k * D + c * 384, 384)]
        one_copies.append(
            push(
                r.qg.at[:, lanes(k * D + (1 - c) * 384, 384)],
                r.rhs1.at[pl.ds(TOK, TOK), pl.ds(k * 384, 384)],
                cp,
            )
        )
    sp.third(0)
    sp.fourth()
    for copy in one_copies + [share_a1, share_at]:
        copy.wait_recv()
    s1.multiply()
    sf.second(3)
    sf.second(1)

    first_grad = jnp.zeros((TOK, D), full)
    for k in range(3):
        first_grad += product_nt(r.qg[:, k * D : (k + 1) * D], w1_cols(k))
    normed = r.normed[...]
    vterm[0:1, :] = jnp.sum(first_grad * normed, axis=0, keepdims=True)
    vterm[1:2, :] = jnp.sum(first_grad, axis=0, keepdims=True)
    vterm[2:3, :] = jnp.sum(r.qg[:, 0:D].astype(full), axis=0, keepdims=True)
    vterm[3:4, :] = jnp.sum(r.qg[:, 2 * D :].astype(full), axis=0, keepdims=True)
    vsend, vrecv = r.vsend, r.vrecv
    vcopy = push(vterm.at[:, lanes((1 - c) * 384, 384)], vrecv.at[0], cp)
    tok_grad = r.resid[...] + norm_back(first_grad, normed, r.inverse[:, 0:1], vector(0))
    tok_out[...] = tok_grad.astype(half)
    sf.third(3)
    vcopy.wait_recv()
    vsend[0] = vterm[:, lanes(c * 384, 384)] + vrecv[0]
    vcopy = push(vsend.at[0], vrecv.at[1], yp)
    sf.second(2)
    sf.third(1)
    sp.fifth()
    for k in range(4):
        block += product(r.hidden[:, k * D : (k + 1) * D], wp_rows(k))
    block_out[...] = block.astype(half)
    sf.second(0)
    sf.third(2)
    vcopy.wait_recv()
    vsend[1] = vsend[0] + vrecv[1]
    vcopy = push(vsend.at[1], vrecv.at[2], xp)
    sf.third(0)
    sf.fourth()
    s1.second(3)
    s1.second(1)
    s1.third(3)
    vcopy.wait_recv()
    vsend[2] = vsend[1] + vrecv[2]
    vcopy = push(vsend.at[2], r.vz.at[0], zp)
    s1.second(2)
    s1.third(1)

    def store_p(owner, value):
        proj_out[:, lanes(owner * 384, 384)] = value

    def store_f(owner, value):
        wide_out[:, lanes(4 * D + owner * F_HALF, F_HALF)] = value

    def store_1(owner, value):
        for k in range(4):
            wide_out[:, lanes(k * D + owner * 384, 384)] = value[:, k * 384 : (k + 1) * 384]

    sp.finish(store_p)
    sf.fifth()
    s1.second(0)
    s1.third(2)
    s1.fourth()
    vcopy.wait_recv()
    r.vz[2] = vsend[2] + r.vz[0]
    vcopy = push(r.vz.at[2], r.vz.at[1], zq)
    s1.third(0)
    vcopy.wait_recv()
    total = r.vz[2] + r.vz[1]
    vsend[3] = total
    vcopy = push(vsend.at[3], vrecv.at[3], cp)
    r.vfull[:, lanes(c * 384, 384)] = total
    sf.finish(store_f)
    s1.fifth()
    vcopy.wait_recv()
    r.vfull[:, lanes((1 - c) * 384, 384)] = vrecv[3]
    shift = D - lax.axis_index("fsdp") * vec.shape[1]
    vec_out[...] = pltpu.roll(r.vfull[...], shift, 1)[0 : vec.shape[0], 0 : vec.shape[1]]
    s1.finish(store_1)
    for copy in sends:
        copy.wait_send()


def block_all(n, tok, lens, cot, wide, proj, vec):
    depth = n // 8
    spaces, parts = scratch_of(depth)
    space = pl.BlockSpec(memory_space=pltpu.VMEM)
    scalars = pl.BlockSpec(memory_space=pltpu.SMEM)
    return pl.pallas_call(
        functools.partial(block_kernel, n, (tuple(spaces), tuple(parts[0]))),
        out_shape=(
            jax.ShapeDtypeStruct((TOK, D), jnp.bfloat16),
            jax.ShapeDtypeStruct((TOK, D), jnp.bfloat16),
            jax.ShapeDtypeStruct((GROUP, 8 * D), jnp.float32),
            jax.ShapeDtypeStruct((P_ROWS, D), jnp.float32),
            jax.ShapeDtypeStruct(vec.shape, jnp.float32),
        ),
        in_specs=[space, scalars, space, space, space, space],
        out_specs=(space,) * 5,
        scratch_shapes=[pltpu.SemaphoreType.DMA((COPIES,))] * 2
        + list(spaces.values())
        + [space for part in parts for space in part.values()],
        compiler_params=pltpu.CompilerParams(
            collective_id=0, has_side_effects=True, vmem_limit_bytes=58 * 2**20
        ),
    )(tok, lens, cot, wide, proj, vec)


def finish_kernel(
    unscale,
    wg,
    pg,
    vg,
    ww,
    pw,
    vw,
    wm,
    pm,
    vm,
    block,
    tok,
    wg_out,
    pg_out,
    vg_out,
    ww_out,
    pw_out,
    vw_out,
    wm_out,
    pm_out,
    vm_out,
    block_out,
    tok_out,
):
    block_out[...] = block[...]
    tok_out[...] = tok[...]
    for grad, old, moment, grad_out, new_out, moment_out, rate, decay in (
        (wg, ww, (wm.at[0], wm.at[1]), wg_out, ww_out, (wm_out.at[0], wm_out.at[1]), rate_matrix, weight_decay),
        (pg, pw, (pm.at[0], pm.at[1]), pg_out, pw_out, (pm_out.at[0], pm_out.at[1]), rate_matrix, weight_decay),
        (vg, vw, (vm.at[:, 0], vm.at[:, 1]), vg_out, vw_out, (vm_out.at[:, 0], vm_out.at[:, 1]), rate_vector, 0.0),
    ):
        gradient = grad[...]
        grad_out[...] = gradient
        scaled_grad = gradient / unscale
        first_moment = beta_one * moment[0][...] + (1.0 - beta_one) * scaled_grad
        second_moment = beta_two * moment[1][...] + (1.0 - beta_two) * scaled_grad * scaled_grad
        corrected_first = first_moment / (1.0 - beta_one**STEP)
        corrected_second = second_moment / (1.0 - beta_two**STEP)
        weights = old[...]
        new_out[...] = weights - rate * (
            corrected_first / (jnp.sqrt(corrected_second) + adam_eps) + decay * weights
        )
        moment_out[0][...] = first_moment
        moment_out[1][...] = second_moment


STEPS = 4


def finish_all(unscale, wg, pg, vg, ww, pw, vw, wm, pm, vm, block, tok):
    vm = vm.transpose(1, 0, 2)
    wide, proj = wg.shape[1] // STEPS, pg.shape[0] // STEPS
    rows, columns = vg.shape
    wide_spec = pl.BlockSpec((GROUP, wide), lambda i: (0, i))
    proj_spec = pl.BlockSpec((proj, D), lambda i: (i, 0))
    vec_spec = pl.BlockSpec((rows, columns), lambda i: (0, 0))
    specs = [wide_spec, proj_spec, vec_spec]
    moments = [
        pl.BlockSpec((2, GROUP, wide), lambda i: (0, 0, i)),
        pl.BlockSpec((2, proj, D), lambda i: (0, i, 0)),
        pl.BlockSpec((rows, 2, columns), lambda i: (0, 0, 0)),
    ]
    flow = [pl.BlockSpec((TOK // STEPS, D), lambda i: (i, 0))] * 2
    arrays = (wg, pg, vg, ww, pw, vw, wm, pm, vm, block, tok)
    shapes = [jax.ShapeDtypeStruct(v.shape, v.dtype) for v in arrays]
    *out, vm, block, tok = pl.pallas_call(
        functools.partial(finish_kernel, unscale),
        grid=(STEPS,),
        out_shape=tuple(shapes),
        in_specs=specs + specs + moments + flow,
        out_specs=tuple(specs + specs + moments + flow),
    )(*arrays)
    return (block, tok, *out, vm.transpose(1, 0, 2))


def body_plain(
    tokens,
    seq_lengths,
    cotangent,
    wide_weights,
    proj_weights,
    vector_params,
    wide_moments,
    proj_moments,
    vector_moments,
):
    shards = (
        wide_weights.astype(jnp.bfloat16),
        proj_weights.astype(jnp.bfloat16),
        vector_params.astype(jnp.bfloat16),
    )
    wide_full, proj_full, vector_full = (
        lax.all_gather(shards[0], "fsdp", axis=0, tiled=True),
        lax.all_gather(shards[1], "fsdp", axis=0, tiled=True),
        lax.all_gather(shards[2], "fsdp", axis=1, tiled=True),
    )
    vectors = vector_full.astype(jnp.float32)
    row_count = tokens.shape[0]
    allowed = allowed_pairs(seq_lengths[0], row_count)
    ratio = FF // D
    local_rows = wide_weights.shape[0]
    unscale = math.sqrt(lax.axis_size("fsdp") * row_count)
    gain_one, shift_one, query_bias, value_bias = (vectors[0], vectors[1], vectors[2], vectors[3])
    out_bias, gain_two, shift_two, proj_bias = (vectors[4], vectors[5], vectors[6], vectors[7])
    fc_bias = vectors[8:].reshape(FF)
    token_float = tokens.astype(jnp.float32)
    first_norm, normed_one, inverse_one = norm_forward(token_float, gain_one, shift_one)
    first_in = first_norm.astype(jnp.bfloat16)
    qkv_bias = jnp.concatenate([query_bias, jnp.zeros_like(query_bias), value_bias])
    qkv_half = (
        jnp.dot(first_in, wide_full[:, : 3 * D], preferred_element_type=jnp.float32) + qkv_bias
    ).astype(jnp.bfloat16)
    queries = qkv_half[:, :D]
    key_rows = qkv_half[:, D : 2 * D]
    value_rows = qkv_half[:, 2 * D :]
    attended, logsum = attention_forward(queries, key_rows, value_rows, allowed)
    residual = (
        token_float
        + jnp.dot(attended, wide_full[:, 3 * D : 4 * D], preferred_element_type=jnp.float32)
        + out_bias
    )
    second_norm, normed_two, inverse_two = norm_forward(residual, gain_two, shift_two)
    second_in = second_norm.astype(jnp.bfloat16)
    before_act = (
        jnp.dot(second_in, wide_full[:, 4 * D :], preferred_element_type=jnp.float32) + fc_bias
    )
    value_part, slope_part = gelu_parts(before_act)
    hidden = value_part.astype(jnp.bfloat16)
    block_output = (
        residual + jnp.dot(hidden, proj_full, preferred_element_type=jnp.float32) + proj_bias
    ).astype(jnp.bfloat16)
    backward_wide, backward_proj, vector_again = wide_full, proj_full, vector_full
    backward_vectors = vector_again.astype(jnp.float32)
    qkv_back = backward_wide[:, : 3 * D]
    out_back = backward_wide[:, 3 * D : 4 * D]
    fc_back = backward_wide[:, 4 * D :]
    cot_float = cotangent.astype(jnp.float32)
    proj_bias_grad = jnp.sum(cot_float, axis=0)
    hidden_grad = jnp.einsum(
        "td,fd->tf", cotangent, backward_proj, preferred_element_type=jnp.float32
    )
    pre_grad = (hidden_grad * slope_part).astype(jnp.bfloat16)
    fc_bias_grad = jnp.sum(pre_grad, axis=0, dtype=jnp.float32)
    second_grad = jnp.einsum("tf,df->td", pre_grad, fc_back, preferred_element_type=jnp.float32)
    resid_norm_grad, gain_two_grad, shift_two_grad = norm_backward(
        second_grad, normed_two, inverse_two, backward_vectors[5]
    )
    resid_grad = cot_float + resid_norm_grad
    mlp_vectors = jnp.concatenate(
        [
            jnp.stack([gain_two_grad, shift_two_grad, proj_bias_grad]),
            fc_bias_grad.reshape(ratio, D),
        ],
        axis=0,
    )
    resid_half = resid_grad.astype(jnp.bfloat16)
    out_bias_grad = jnp.sum(resid_grad, axis=0)
    attended_grad = jnp.einsum(
        "te,de->td", resid_half, out_back, preferred_element_type=jnp.float32
    ).astype(jnp.bfloat16)
    qkv_grad = attention_backward(queries, key_rows, value_rows, allowed, logsum, attended_grad)
    query_bias_grad = jnp.sum(qkv_grad[:, :D], axis=0, dtype=jnp.float32)
    value_bias_grad = jnp.sum(qkv_grad[:, 2 * D :], axis=0, dtype=jnp.float32)
    first_grad = jnp.einsum("tc,dc->td", qkv_grad, qkv_back, preferred_element_type=jnp.float32)
    token_norm_grad, gain_one_grad, shift_one_grad = norm_backward(
        first_grad, normed_one, inverse_one, backward_vectors[0]
    )
    tokens_grad = (resid_grad + token_norm_grad).astype(jnp.bfloat16)
    attn_vectors = jnp.stack(
        [gain_one_grad, shift_one_grad, query_bias_grad, value_bias_grad, out_bias_grad]
    )
    vector_terms = jnp.concatenate([attn_vectors, mlp_vectors], axis=0)
    fc_part = column_term(second_in, pre_grad)
    proj_part = column_term(hidden, cotangent).reshape(
        local_rows * lax.axis_size("fsdp"), ratio * D
    )
    qkv_part = column_term(first_in, qkv_grad)
    out_part = column_term(attended, resid_half)
    joined_shard = lax.psum_scatter(
        jnp.concatenate(
            [
                jnp.concatenate([qkv_part, out_part], axis=1),
                jnp.concatenate([fc_part, proj_part], axis=1),
            ],
            axis=1,
        ),
        "fsdp",
        scatter_dimension=0,
        tiled=True,
    )
    wide_grad = joined_shard[:, : 4 * D + FF]
    proj_grad = joined_shard[:, 4 * D + FF :].reshape(local_rows * ratio, D)
    vector_grad = lax.psum_scatter(vector_terms, "fsdp", scatter_dimension=1, tiled=True)
    wide_new, wide_moments_new = adam_update(
        wide_weights, wide_moments, wide_grad, rate_matrix, weight_decay, unscale
    )
    proj_new, proj_moments_new = adam_update(
        proj_weights, proj_moments, proj_grad, rate_matrix, weight_decay, unscale
    )
    vector_new, vector_moments_new = adam_update(
        vector_params, vector_moments, vector_grad, rate_vector, 0.0, unscale
    )
    return (
        block_output,
        tokens_grad,
        wide_grad,
        proj_grad,
        vector_grad,
        wide_new,
        proj_new,
        vector_new,
        wide_moments_new,
        proj_moments_new,
        vector_moments_new,
    )


def body(
    tokens,
    seq_lengths,
    cotangent,
    wide_weights,
    proj_weights,
    vector_params,
    wide_moments,
    proj_moments,
    vector_moments,
):
    n = lax.axis_size("fsdp")
    if not (n == 32 and wide_weights.shape[0] == GROUP and tokens.shape[0] == TOK):
        return body_plain(
            tokens,
            seq_lengths,
            cotangent,
            wide_weights,
            proj_weights,
            vector_params,
            wide_moments,
            proj_moments,
            vector_moments,
        )
    block_output, tokens_grad, wide_grad, proj_grad, vector_sum = block_all(
        n, tokens, seq_lengths, cotangent, wide_weights, proj_weights, vector_params
    )
    unscale = math.sqrt(n * tokens.shape[0])
    results = finish_all(
        unscale,
        wide_grad,
        proj_grad,
        vector_sum,
        wide_weights,
        proj_weights,
        vector_params,
        wide_moments,
        proj_moments,
        vector_moments,
        block_output,
        tokens_grad,
    )
    return results


def solution(mesh):
    placed = (
        P("fsdp", None),
        P("fsdp", None),
        P("fsdp", None),
        P("fsdp", None),
        P("fsdp", None),
        P(None, "fsdp"),
        P(None, "fsdp", None),
        P(None, "fsdp", None),
        P(None, None, "fsdp"),
    )
    return jax.shard_map(
        body,
        mesh=mesh,
        in_specs=placed,
        out_specs=(
            P("fsdp", None),
            P("fsdp", None),
            P("fsdp", None),
            P("fsdp", None),
            P(None, "fsdp"),
            P("fsdp", None),
            P("fsdp", None),
            P(None, "fsdp"),
            P(None, "fsdp", None),
            P(None, "fsdp", None),
            P(None, None, "fsdp"),
        ),
        check_vma=False,
    )
```

```python
import functools
import math
import types

import jax
import jax.numpy as jnp
from jax import lax
from jax.experimental import pallas as pl
from jax.experimental.pallas import tpu as pltpu
from jax.sharding import PartitionSpec as P

D = 768
H = 12
HD = 64
FF = 3072
STEP = 2


norm_eps = 1e-05
beta_one = 0.9
beta_two = 0.95
adam_eps = 1e-08
rate_matrix = 0.02
rate_vector = 0.2
weight_decay = 0.1
gelu_coeff = 0.7978845608028654
masked_score = -1e30


def norm_forward(values, gain_row, offset):
    center = values - jnp.mean(values, axis=1, keepdims=True)
    variance = jnp.mean(center * center, axis=1, keepdims=True)
    inverse = lax.rsqrt(variance + norm_eps)
    normed = center * inverse
    return (normed * gain_row + offset, normed, inverse)


def norm_backward(upstream, normed, inverse, gain_row):
    scaled = upstream * gain_row
    mean_term = jnp.mean(scaled, axis=1, keepdims=True)
    proj_term = jnp.mean(scaled * normed, axis=1, keepdims=True)
    input_grad = inverse * (scaled - mean_term - normed * proj_term)
    return (input_grad, jnp.sum(upstream * normed, axis=0), jnp.sum(upstream, axis=0))


def gelu_parts(before):
    inner_arg = gelu_coeff * (before + 0.044715 * before * before * before)
    tangent = jnp.tanh(inner_arg)
    value_part = 0.5 * before * (1.0 + tangent)
    slope_part = 0.5 * (1.0 + tangent) + 0.5 * before * (1.0 - tangent * tangent) * gelu_coeff * (
        1.0 + 3.0 * 0.044715 * before * before
    )
    return (value_part, slope_part)


def allowed_pairs(length_row, row_count):
    order = jnp.arange(length_row.shape[0], dtype=jnp.int32)
    bounds = jnp.sum(jnp.where(order[None, :] <= order[:, None], length_row[None, :], 0), axis=1)
    position = jnp.arange(row_count, dtype=jnp.int32)
    segment = jnp.sum((position[:, None] >= bounds[None, :]).astype(jnp.int32), axis=1)
    return (segment[:, None] == segment[None, :]) & (position[None, :] <= position[:, None])


def head_view(matrix):
    return matrix.reshape(matrix.shape[0], H, HD)


def score_table(queries, key_rows, allowed):
    scale_factor = 1.0 / math.sqrt(HD)
    scores = (
        jnp.einsum(
            "qhd,khd->hqk",
            head_view(queries),
            head_view(key_rows),
            preferred_element_type=jnp.float32,
        )
        * scale_factor
    )
    return jnp.where(allowed[None, :, :], scores, masked_score)


def attention_forward(queries, key_rows, value_rows, allowed):
    scores = score_table(queries, key_rows, allowed)
    highest = jnp.max(scores, axis=2, keepdims=True)
    logsum = highest + jnp.log(jnp.sum(jnp.exp(scores - highest), axis=2, keepdims=True))
    weights = jnp.exp(scores - logsum).astype(jnp.bfloat16)
    mixed = jnp.einsum(
        "hqk,khd->qhd", weights, head_view(value_rows), preferred_element_type=jnp.float32
    )
    return (mixed.reshape(queries.shape[0], D).astype(jnp.bfloat16), logsum)


def attention_backward(queries, key_rows, value_rows, allowed, logsum, upstream):
    scale_factor = 1.0 / math.sqrt(HD)
    scores = score_table(queries, key_rows, allowed)
    probs = jnp.exp(scores - logsum)
    rounded = probs.astype(jnp.bfloat16)
    grad_heads = head_view(upstream)
    value_grad = jnp.einsum("hqk,qhd->khd", rounded, grad_heads, preferred_element_type=jnp.float32)
    prob_grad = jnp.einsum(
        "qhd,khd->hqk", grad_heads, head_view(value_rows), preferred_element_type=jnp.float32
    )
    delta_row = jnp.sum(probs * prob_grad, axis=2, keepdims=True)
    score_grad = (probs * (prob_grad - delta_row) * scale_factor).astype(jnp.bfloat16)
    query_grad = jnp.einsum(
        "hqk,khd->qhd", score_grad, head_view(key_rows), preferred_element_type=jnp.float32
    )
    key_grad = jnp.einsum(
        "hqk,qhd->khd", score_grad, head_view(queries), preferred_element_type=jnp.float32
    )
    row_total = queries.shape[0]
    joined = jnp.concatenate(
        [
            query_grad.reshape(row_total, D),
            key_grad.reshape(row_total, D),
            value_grad.reshape(row_total, D),
        ],
        axis=1,
    )
    return joined.astype(jnp.bfloat16)


def adam_update(weights, moments, gradient, rate, decay_rate, unscale):
    scaled_grad = gradient / unscale
    first_moment = beta_one * moments[0] + (1.0 - beta_one) * scaled_grad
    second_moment = beta_two * moments[1] + (1.0 - beta_two) * scaled_grad * scaled_grad
    corrected_first = first_moment / (1.0 - beta_one**STEP)
    corrected_second = second_moment / (1.0 - beta_two**STEP)
    updated = weights - rate * (
        corrected_first / (jnp.sqrt(corrected_second) + adam_eps) + decay_rate * weights
    )
    return (updated, jnp.stack([first_moment, second_moment]))


def column_term(left, right):
    return jnp.einsum("tc,te->ce", left, right, preferred_element_type=jnp.float32)


MESH = pl.DeviceIdType.MESH
GROUP = 24


def position(n):
    depth = n // 8
    me = lax.axis_index("fsdp")
    return depth, me // 8, (me // 4) % 2, (me // 2) % 2, me % 2


def device_at(z, y, x, c):
    return ((z * 2 + y) * 2 + x) * 2 + c


def greet(partners):
    barrier = pltpu.get_barrier_semaphore()
    for device in partners:
        pl.semaphore_signal(barrier, inc=1, device_id=(device,), device_id_type=MESH)
    pl.semaphore_wait(barrier, len(partners))


def remote(src, dst, send, recv, device):
    return pltpu.make_async_remote_copy(
        src_ref=src,
        dst_ref=dst,
        send_sem=send,
        recv_sem=recv,
        device_id=(device,),
        device_id_type=MESH,
    )


def product(left, right):
    return jnp.dot(left, right, preferred_element_type=jnp.float32)


def product_nt(left, right):
    return lax.dot_general(
        left, right, (((1,), (1,)), ((), ())), preferred_element_type=jnp.float32
    )


def product_tn(left, right):
    return lax.dot_general(
        left, right, (((0,), (0,)), ((), ())), preferred_element_type=jnp.float32
    )


TOK = 128
UNIT = 2 * GROUP
W1 = 4 * D + 256
W1_HALF = W1 // 2
W1_FIRST = 1024
F_HALF = FF // 2
F_FIRST = 1024
P_ROWS = FF // 32
P_FIRST = 64
ROWS_OF = (2 * P_ROWS, UNIT, UNIT)
FIRST_OF = (256, 1024, 896)
WIDTH_OF = (384, 1536, 1536)


def scratch_of(depth):
    half, full = jnp.bfloat16, jnp.float32

    def vmem(shape, dtype):
        return pltpu.VMEM(shape, dtype)

    lead = (depth, 2, 2)
    spaces = dict(
        ext=vmem((32, 4 * D + 256 + FF), half),
        ext_in=vmem((32, 4 * D + 256 + FF), half),
        w1=vmem(lead + (UNIT, W1), half),
        wf=vmem(lead + (UNIT, FF), half),
        wp=vmem(lead + (2 * P_ROWS, D), half),
        vecs=vmem((16, D + 128), full),
        normed=vmem((TOK, D), full),
        inverse=vmem((TOK, 128), full),
        normed2=vmem((TOK, D), full),
        inverse2=vmem((TOK, 128), full),
        allowed=vmem((TOK, TOK), full),
        window=vmem((GROUP, 256), full),
        qkv=vmem((TOK, 3 * D), half),
        probs=vmem((H, TOK, TOK), full),
        mixed=vmem((TOK, D), half),
        resid=vmem((TOK, D), full),
        second=vmem((TOK, D), half),
        slope=vmem((TOK, FF), full),
        hidden=vmem((TOK, FF), half),
        pre=vmem((TOK, FF), half),
        up=vmem((TOK, D), half),
        qg=vmem((TOK, 3 * D), half),
        a1t=vmem(lead + (UNIT, 2 * TOK), half),
        att=vmem(lead + (UNIT, 2 * TOK), half),
        a2t=vmem(lead + (UNIT, 2 * TOK), half),
        hidt=vmem(lead + (2 * P_ROWS, 2 * TOK), half),
        rhsp=vmem((2 * TOK, 384), half),
        rhsf=vmem((2 * TOK, F_HALF), half),
        rhs1=vmem((2 * TOK, 4 * 384), half),
        vterm=vmem((16, D), full),
        vfull=vmem((16, D), full),
        vsend=vmem((4, 16, 384), full),
        vrecv=vmem((4, 16, 384), full),
        vz=vmem((depth - 1, 16, 384), full),
    )
    parts = []
    for k in range(3):
        rows, first, width = ROWS_OF[k], FIRST_OF[k], WIDTH_OF[k]
        rest = width - first
        parts.append(
            dict(
                give_a=vmem((depth, 2, rows, first), half),
                land_a=vmem((depth, 2, rows, first), half),
                keep_a=vmem((depth, 2, rows, first), full),
                give_b=vmem((depth, 2, rows, rest), half),
                land_b=vmem((depth, 2, rows, rest), half),
                keep_b=vmem((depth, 2, rows, rest), full),
                sa2=vmem((depth, rows, first), half),
                ra2=vmem((depth, rows, first), half),
                sa3=vmem((depth, rows, first), half),
                ra3=vmem((depth - 1, rows, first), half),
                sb2=vmem((depth, 2, rows, rest), half),
                rb2=vmem((depth - 1, 2, rows, rest), half),
                sb3=vmem((rows, rest), half),
                rb3=vmem((rows, rest), half),
                fin=vmem((rows, width), full),
                rfin=vmem((rows // 2, width), full),
            )
        )
    return spaces, parts


COPIES = 232


def block_kernel(n, names, tok, lens, cot, wide, proj, vec, block_out, tok_out, wide_out, proj_out, vec_out, *refs):
    names, part_names = names
    ssem, rsem = refs[0], refs[1]
    r = types.SimpleNamespace(**dict(zip(names, refs[2:])))
    part_refs = []
    for k in range(3):
        first = 2 + len(names) + k * len(part_names)
        part_refs.append(types.SimpleNamespace(**dict(zip(part_names, refs[first:]))))
    depth, z, y, x, c = position(n)
    z_pair, z_far = z + 1 - 2 * (z % 2), depth - 1 - z
    z_units = (z, z_pair, z_far, depth - 1 - z_pair)
    zp, zq = device_at(z_pair, y, x, c), device_at(z_far, y, x, c)
    yp, xp = device_at(z, 1 - y, x, c), device_at(z, y, 1 - x, c)
    cp = device_at(z, y, x, 1 - c)
    half, full = jnp.bfloat16, jnp.float32
    sends = []
    count = [0]

    def push(src, dst, device, landed=None):
        k = count[0]
        count[0] = k + 1
        copy = remote(src, dst, ssem.at[k], rsem.at[k], device)
        copy.start()
        sends.append(copy)
        landed = dst if landed is None else landed
        return remote(landed, landed, ssem.at[k], rsem.at[k], device)

    def lanes(start, size):
        return pl.ds(pl.multiple_of(start, 128), size)

    wide_now = wide[...].astype(half).astype(full)
    r.window[...] = jnp.zeros((GROUP, 256), full)
    r.window[0 : vec.shape[0], 0 : vec.shape[1]] = vec[...]
    shift = lax.rem(lax.axis_index("fsdp") * vec.shape[1], 128)
    vec_now = pltpu.roll(r.window[...], shift, 1)
    r.ext[0:GROUP, 0 : 4 * D] = wide_now[:, 0 : 4 * D].astype(half)
    r.ext[0:GROUP, 4 * D : W1] = vec_now.astype(half)
    r.ext[0:GROUP, W1:] = wide_now[:, 4 * D :].astype(half)
    r.ext[GROUP:, :] = jnp.zeros((32 - GROUP, W1 + FF), half)
    r.wp[z, y, x, pl.ds(pl.multiple_of(c * P_ROWS, 32), P_ROWS), :] = proj[...].astype(half)
    greet([zp, zq, yp, xp, cp])
    ext_copy = push(r.ext, r.ext_in, cp)

    def w1_at(s):
        start = c * W1_HALF + (W1_FIRST if s else 0)
        size = W1_HALF - W1_FIRST if s else W1_FIRST
        return lambda zi, yi, xi: r.w1.at[zi, yi, xi, :, lanes(start, size)]

    def wf_at(s):
        start = c * F_HALF + (F_FIRST if s else 0)
        size = F_HALF - F_FIRST if s else F_FIRST
        return lambda zi, yi, xi: r.wf.at[zi, yi, xi, :, lanes(start, size)]

    def wp_at(s):
        start = c * P_ROWS + (P_FIRST if s else 0)
        size = P_ROWS - P_FIRST if s else P_FIRST
        return lambda zi, yi, xi: r.wp.at[zi, yi, xi, pl.ds(pl.multiple_of(start, 32), size), :]

    every, both = pl.ds(0, depth), pl.ds(0, 2)

    def zat(d):
        return z_units[d]

    class Gather:
        def __init__(self, a, b, own):
            self.a, self.b, self.own = a, b, own
            self.cores = []

        def core(self, ref, landed):
            self.cores.append((ref, landed))

        def start(self):
            a, b = self.a, self.b
            mine_a, mine_b = a(z, y, x), b(z, y, x)
            self.by = push(mine_b, mine_b, yp, b(z, 1 - y, x))
            self.az, self.bz, self.ax, self.ay, self.bx = {}, {}, {}, {}, {}
            self.ax[0] = push(mine_a, mine_a, xp, a(z, y, 1 - x))
            self.ay[0, 0] = push(mine_a, mine_a, yp, a(z, 1 - y, x))
            self.bx[0, 0] = push(mine_b, mine_b, xp, b(z, y, 1 - x))
            self.done = []
            if self.own:
                self.done.append(push(mine_a, mine_a, cp, OWN_A(z, y, x)))
                self.done.append(push(mine_b, mine_b, cp, OWN_B(z, y, x)))

        def start_z(self):
            a, b = self.a, self.b
            mine_a, mine_b = a(z, y, x), b(z, y, x)
            for d, device in ((2, zq), (1, zp)):
                self.az[d] = push(mine_a, mine_a, device, a(zat(d), y, x))
            for d, device in ((2, zq), (1, zp)):
                self.bz[d, 0] = push(mine_b, mine_b, device, b(zat(d), y, x))

        def first(self):
            b = self.b
            self.by.wait_recv()
            got = b(z, 1 - y, x)
            for d, device in ((2, zq), (1, zp)):
                self.bz[d, 1] = push(got, got, device, b(zat(d), 1 - y, x))
            self.bx[0, 1] = push(got, got, xp, b(z, 1 - y, 1 - x))
            self.give(b, (z, 1 - y, x))

        def give(self, at, where):
            ref = at(*where)
            self.done.append(push(ref, ref, cp, (PEER_A if at is self.a else PEER_B)[id(self)](*where)))

        def near(self, d):
            a = self.a
            self.az[d].wait_recv()
            got = a(zat(d), y, x)
            if d == 2:
                self.az[3] = push(got, got, zp, a(zat(3), y, x))
            self.ax[d] = push(got, got, xp, a(zat(d), y, 1 - x))
            self.ay[0, d] = push(got, got, yp, a(zat(d), 1 - y, x))
            self.give(a, (zat(d), y, x))

        def side(self, d):
            a = self.a
            self.ax[d].wait_recv()
            got = a(zat(d), y, 1 - x)
            self.ay[1, d] = push(got, got, yp, a(zat(d), 1 - y, 1 - x))

        def side_done(self):
            self.give(self.a, (every, y, 1 - x))

        def deep(self, d):
            b = self.b
            for k, yi in ((0, y), (1, 1 - y)):
                self.bz[d, k].wait_recv()
                got = b(zat(d), yi, x)
                if d == 2:
                    self.bz[3, k] = push(got, got, zp, b(zat(3), yi, x))
                self.bx[d, k] = push(got, got, xp, b(zat(d), yi, 1 - x))
            self.give(b, (zat(d), both, x))

        def last(self):
            for d in (0, 2, 1, 3):
                self.bx[d, 0].wait_recv()
                self.bx[d, 1].wait_recv()
                self.give(self.b, (zat(d), both, 1 - x))
            for d in (0, 2, 1, 3):
                self.ay[0, d].wait_recv()
                self.ay[1, d].wait_recv()
                self.give(self.a, (zat(d), 1 - y, both))

        def finish(self):
            for copy in self.done:
                copy.wait_recv()

    PEER_A, PEER_B = {}, {}

    def peer_at(ref, cut, start_of, size):
        start = start_of(1 - c)
        if cut == "lanes":
            return lambda zi, yi, xi: ref.at[zi, yi, xi, :, lanes(start, size)]
        return lambda zi, yi, xi: ref.at[zi, yi, xi, pl.ds(pl.multiple_of(start, 32), size), :]

    g1 = Gather(w1_at(0), w1_at(1), False)
    gf = Gather(wf_at(0), wf_at(1), False)
    gp = Gather(wp_at(0), wp_at(1), True)
    for g, ref, cut, whole, cut_at in (
        (g1, r.w1, "lanes", W1_HALF, W1_FIRST),
        (gf, r.wf, "lanes", F_HALF, F_FIRST),
        (gp, r.wp, "rows", P_ROWS, P_FIRST),
    ):
        PEER_A[id(g)] = peer_at(ref, cut, lambda k, w=whole: k * w, cut_at)
        PEER_B[id(g)] = peer_at(ref, cut, lambda k, w=whole, o=cut_at: k * w + o, whole - cut_at)
    OWN_A, OWN_B = PEER_A[id(gp)], PEER_B[id(gp)]

    token_float = tok[...].astype(full)
    center = token_float - jnp.mean(token_float, axis=1, keepdims=True)
    inverse = lax.rsqrt(jnp.mean(center * center, axis=1, keepdims=True) + norm_eps)
    r.normed[...] = center * inverse
    r.inverse[...] = jnp.broadcast_to(inverse, (TOK, 128))
    across = lax.broadcasted_iota(jnp.int32, (TOK, TOK), 1)
    down = lax.broadcasted_iota(jnp.int32, (TOK, TOK), 0)
    seg_across = jnp.zeros((TOK, TOK), jnp.int32)
    seg_down = jnp.zeros((TOK, TOK), jnp.int32)
    bound = 0
    for j in range(lens.shape[1]):
        bound = bound + lens[0, j]
        seg_across += (across >= bound).astype(jnp.int32)
        seg_down += (down >= bound).astype(jnp.int32)
    r.allowed[...] = ((seg_across == seg_down) & (across <= down)).astype(full)

    ext_copy.wait_recv()

    def assemble(target, start, size):
        for o in range(0, size, 512):
            w = min(512, size - o)
            mine = r.ext[:, start + o : start + o + w].astype(full)[:GROUP]
            theirs = r.ext_in[:, start + o : start + o + w].astype(full)[:GROUP]
            low = jnp.where(c == 0, mine, theirs)
            high = jnp.where(c == 0, theirs, mine)
            target[z, y, x, :, o : o + w] = jnp.concatenate([low, high], axis=0).astype(half)

    assemble(r.w1, 0, W1)
    g1.start()
    g1.start_z()
    assemble(r.wf, W1, FF)
    gf.start()
    gp.start()
    cot_copy = push(cot.at[:, lanes((1 - c) * 384, 384)], r.rhsp.at[pl.ds(TOK, TOK), :], cp)
    r.rhsp[0:TOK, :] = cot[:, lanes(c * 384, 384)]
    g1.first()
    g1.near(2)
    gf.start_z()
    gf.first()
    g1.side(0)
    g1.near(1)
    g1.side(2)
    g1.deep(2)
    g1.near(3)
    g1.side(1)
    g1.side(3)
    g1.side_done()
    g1.deep(1)
    g1.deep(3)
    gf.near(2)
    gp.start_z()
    gp.first()
    gf.side(0)
    g1.last()
    gf.near(1)
    g1.finish()

    r.vecs[...] = jnp.zeros((16, D + 128), full)
    for chip in range(n // 2):
        block = r.w1[chip // 4, (chip // 2) % 2, chip % 2, :, 4 * D : W1].astype(full)
        for core in range(2):
            first = ((2 * chip + core) * GROUP) // 128 * 128
            r.vecs[0:16, first : first + 256] += block[core * GROUP : core * GROUP + 16]

    def vector(k):
        return r.vecs[k : k + 1, 0:D]

    def w1_cols(k):
        return r.w1[:, :, :, :, k * D : (k + 1) * D].reshape(D, D)

    def wf_cols(k):
        return r.wf[:, :, :, :, k * D : (k + 1) * D].reshape(D, D)

    def wp_rows(k):
        return r.wp[k : k + 1].reshape(FF // depth, D)

    def transpose_half(value):
        return value.astype(full).T.astype(half)

    def share(ref, value):
        ref[:, :, :, :, 0:TOK] = transpose_half(value).reshape(ref.shape[:4] + (TOK,))
        return push(ref.at[:, :, :, :, pl.ds(0, TOK)], ref.at[:, :, :, :, pl.ds(TOK, TOK)], cp)

    first_in = (r.normed[...] * vector(0) + vector(1)).astype(half)

    def qkv_chunk(k):
        value = product(first_in, w1_cols(k))
        if k != 1:
            value = value + vector(2 if k == 0 else 3)
        r.qkv[:, k * D : (k + 1) * D] = value.astype(half)

    qkv_chunk(0)
    gf.side(2)
    gf.near(3)
    qkv_chunk(1)
    gf.side(1)
    qkv_chunk(2)
    gf.deep(2)
    gf.side(3)
    gf.side_done()

    scale = 1.0 / math.sqrt(HD)

    def head_forward(h):
        lo = h * HD
        q, k = r.qkv[:, lo : lo + HD], r.qkv[:, D + lo : D + lo + HD]
        v = r.qkv[:, 2 * D + lo : 2 * D + lo + HD]
        scores = jnp.where(r.allowed[...] > 0.5, product_nt(q, k) * scale, masked_score)
        highest = jnp.max(scores, axis=1, keepdims=True)
        raised = jnp.exp(scores - highest)
        probs = raised / jnp.sum(raised, axis=1, keepdims=True)
        r.probs[h] = probs
        r.mixed[:, lo : lo + HD] = product(probs.astype(half), v).astype(half)

    for h in range(0, 3):
        head_forward(h)
    gf.deep(1)
    for h in range(3, 6):
        head_forward(h)
    gf.deep(3)
    for h in range(6, 9):
        head_forward(h)
    gp.near(2)
    gp.side(0)
    for h in range(9, H):
        head_forward(h)
    gp.near(1)
    gp.side(2)

    residual = tok[...].astype(full) + product(r.mixed[...], w1_cols(3)) + vector(4)
    r.resid[...] = residual
    center = residual - jnp.mean(residual, axis=1, keepdims=True)
    inverse = lax.rsqrt(jnp.mean(center * center, axis=1, keepdims=True) + norm_eps)
    normed = center * inverse
    r.normed2[...] = normed
    r.inverse2[...] = jnp.broadcast_to(inverse, (TOK, 128))
    r.second[...] = (normed * vector(5) + vector(6)).astype(half)
    gf.last()
    gp.near(3)
    gp.side(1)
    share_at = share(r.att, r.mixed[...])
    share_a1 = share(r.a1t, first_in)
    share_a2 = share(r.a2t, r.second[...])
    gf.finish()

    shares = {}

    def hidden_chunk(k):
        cols = pl.ds(k * D, D)
        before = product(r.second[...], wf_cols(k)) + vector(8 + k)
        value_part, slope_part = gelu_parts(before)
        r.slope[:, cols] = slope_part
        act = value_part.astype(half)
        r.hidden[:, cols] = act
        piece = r.hidt.at[pl.ds(k, 1)]
        r.hidt[k : k + 1, :, :, :, 0:TOK] = transpose_half(act).reshape(1, 2, 2, 2 * P_ROWS, TOK)
        shares[k] = push(piece.at[:, :, :, :, pl.ds(0, TOK)], piece.at[:, :, :, :, pl.ds(TOK, TOK)], cp)

    hidden_chunk(0)
    gp.side(3)
    gp.side_done()
    gp.deep(2)
    hidden_chunk(1)
    hidden_chunk(2)
    gp.deep(1)
    hidden_chunk(3)

    class Scatter:
        def __init__(self, k, dots):
            self.r = part_refs[k]
            self.rows, self.cut, self.width = ROWS_OF[k], FIRST_OF[k], WIDTH_OF[k]
            self.dots = dots
            self.a1, self.b1, self.a2, self.b2, self.a3 = {}, {}, {}, {}, {}

        def give_y(self):
            give = self.r.give_a
            for d in (3, 1, 2, 0):
                u = z_units[d]
                value = self.dots(0, lambda ref: ref[u, 1 - y]).astype(half)
                give[u] = value.reshape(2, self.rows, self.cut)
                self.a1[d, 1] = push(give.at[u, 1 - x], self.r.land_a.at[u, 1 - x], yp)
            for d in (3, 1, 2, 0):
                u = z_units[d]
                self.a1[d, 0] = push(give.at[u, x], self.r.land_a.at[u, x], yp)

        def give_x(self):
            give = self.r.give_b
            for d in (3, 1, 2, 0):
                u = z_units[d]
                value = self.dots(1, lambda ref: ref[u, :, 1 - x]).astype(half)
                give[u] = value.reshape(2, self.rows, self.width - self.cut)
                self.b1[d] = push(give.at[u], self.r.land_b.at[u], xp)

        def keep(self):
            for d in (3, 1, 2, 0):
                u = z_units[d]
                value = self.dots(0, lambda ref: ref[u, y])
                self.r.keep_a[u] = value.reshape(2, self.rows, self.cut)
                value = self.dots(1, lambda ref: ref[u, :, x])
                self.r.keep_b[u] = value.reshape(2, self.rows, self.width - self.cut)

        def multiply(self):
            self.give_y()
            self.give_x()
            self.keep()

        def second(self, d):
            u = z_units[d]
            self.a1[d, 1].wait_recv()
            keep, land = self.r.keep_a, self.r.land_a
            self.r.sa2[u] = (keep[u, 1 - x] + land[u, 1 - x].astype(full)).astype(half)
            self.a2[d] = push(self.r.sa2.at[u], self.r.ra2.at[u], xp)
            self.b1[d].wait_recv()
            keep, land = self.r.keep_b, self.r.land_b
            total = keep[u] + land[u].astype(full)
            if d == 2:
                self.b2[3].wait_recv()
                total += self.r.rb2[2].astype(full)
            if d:
                self.r.sb2[u] = total.astype(half)
                self.b2[d] = push(self.r.sb2.at[u], self.r.rb2.at[d - 1], zq if d == 2 else zp)
            else:
                keep[u] = total

        def third(self, d):
            u = z_units[d]
            self.a2[d].wait_recv()
            self.a1[d, 0].wait_recv()
            total = (
                self.r.keep_a[u, x]
                + self.r.land_a[u, x].astype(full)
                + self.r.ra2[u].astype(full)
            )
            if d == 2:
                self.a3[3].wait_recv()
                total += self.r.ra3[2].astype(full)
            if d:
                self.r.sa3[u] = total.astype(half)
                self.a3[d] = push(self.r.sa3.at[u], self.r.ra3.at[d - 1], zq if d == 2 else zp)
            else:
                self.r.fin[:, 0 : self.cut] = total

        def fourth(self):
            keep = self.r.keep_b
            total = keep[z]
            for d in (1, 2):
                self.b2[d].wait_recv()
                total += self.r.rb2[d - 1].astype(full)
            keep[z] = total
            self.r.sb3[...] = keep[z, 1 - y].astype(half)
            self.b3 = push(self.r.sb3, self.r.rb3, yp)

        def fifth(self):
            fin = self.r.fin
            total = fin[:, 0 : self.cut]
            for d in (1, 2):
                self.a3[d].wait_recv()
                total += self.r.ra3[d - 1].astype(full)
            fin[:, 0 : self.cut] = total
            self.b3.wait_recv()
            fin[:, self.cut :] = self.r.keep_b[z, y] + self.r.rb3[...].astype(full)
            size = self.rows // 2
            theirs = pl.ds(pl.multiple_of((1 - c) * size, 8), size)
            self.swap = push(fin.at[theirs, :], self.r.rfin, cp)

        def finish(self, store):
            size = self.rows // 2
            store(c, self.r.fin[pl.ds(pl.multiple_of(c * size, 8), size), :])
            self.swap.wait_recv()
            store(1 - c, self.r.rfin[...])

    def flat(value):
        return value.reshape(-1, 2 * TOK)

    def dots_p(s, pick):
        left = flat(pick(r.hidt))
        return product(left, r.rhsp[:, 256:384] if s else r.rhsp[:, 0:256])

    def dots_f(s, pick):
        left = flat(pick(r.a2t))
        return product(left, r.rhsf[:, 1024:1536] if s else r.rhsf[:, 0:1024])

    def dots_1(s, pick):
        left = flat(pick(r.a1t))
        if s == 0:
            return product(left, r.rhs1[:, 0:896])
        part = product(left, r.rhs1[:, 896:1152])
        return jnp.concatenate([part, product(flat(pick(r.att)), r.rhs1[:, 1152:1536])], axis=1)

    cot_copy.wait_recv()
    for k in range(4):
        shares[k].wait_recv()
    sp, sf, s1 = Scatter(0, dots_p), Scatter(1, dots_f), Scatter(2, dots_1)
    gp.deep(3)
    sp.multiply()
    gp.last()
    gp.finish()

    vterm = r.vterm
    vterm[...] = jnp.zeros((16, D), full)
    vterm[7:8, :] = jnp.sum(cot[...].astype(full), axis=0, keepdims=True)
    second_grad = jnp.zeros((TOK, D), full)
    for k in range(4):
        cols = pl.ds(k * D, D)
        grad = (product_nt(cot[...], wp_rows(k)) * r.slope[:, cols]).astype(half)
        r.pre[:, cols] = grad
        vterm[8 + k : 9 + k, :] = jnp.sum(grad.astype(full), axis=0, keepdims=True)
    r.rhsf[0:TOK, :] = r.pre[:, lanes(c * F_HALF, F_HALF)]
    pre_copy = push(
        r.pre.at[:, lanes((1 - c) * F_HALF, F_HALF)], r.rhsf.at[pl.ds(TOK, TOK), :], cp
    )
    sp.second(3)
    sp.second(1)
    pre_copy.wait_recv()
    share_a2.wait_recv()
    sf.multiply()
    for k in range(4):
        second_grad += product_nt(r.pre[:, k * D : (k + 1) * D], wf_cols(k))

    def norm_back(upstream, normed, inverse, gain):
        scaled = upstream * gain
        mean_term = jnp.mean(scaled, axis=1, keepdims=True)
        proj_term = jnp.mean(scaled * normed, axis=1, keepdims=True)
        return inverse * (scaled - mean_term - normed * proj_term)

    normed = r.normed2[...]
    vterm[5:6, :] = jnp.sum(second_grad * normed, axis=0, keepdims=True)
    vterm[6:7, :] = jnp.sum(second_grad, axis=0, keepdims=True)
    resid_grad = cot[...].astype(full) + norm_back(
        second_grad, normed, r.inverse2[:, 0:1], vector(5)
    )
    block = r.resid[...] + vector(7)
    r.resid[...] = resid_grad
    resid_half = resid_grad.astype(half)
    r.up[...] = resid_half
    vterm[4:5, :] = jnp.sum(resid_grad, axis=0, keepdims=True)
    r.rhs1[0:TOK, 1152:1536] = r.up[:, lanes(c * 384, 384)]
    one_copies = [
        push(
            r.up.at[:, lanes((1 - c) * 384, 384)],
            r.rhs1.at[pl.ds(TOK, TOK), pl.ds(1152, 384)],
            cp,
        )
    ]
    attended_grad = product_nt(resid_half, w1_cols(3)).astype(half)
    r.mixed[...] = attended_grad

    def head_backward(h):
        lo = h * HD
        q, k = r.qkv[:, lo : lo + HD], r.qkv[:, D + lo : D + lo + HD]
        v = r.qkv[:, 2 * D + lo : 2 * D + lo + HD]
        grad = r.mixed[:, lo : lo + HD]
        probs = r.probs[h]
        value_grad = product_tn(probs.astype(half), grad)
        prob_grad = product_nt(grad, v)
        delta = jnp.sum(probs * prob_grad, axis=1, keepdims=True)
        score_grad = (probs * (prob_grad - delta) * scale).astype(half)
        r.qg[:, lo : lo + HD] = product(score_grad, k).astype(half)
        r.qg[:, D + lo : D + lo + HD] = product_tn(score_grad, q).astype(half)
        r.qg[:, 2 * D + lo : 2 * D + lo + HD] = value_grad.astype(half)

    sp.second(2)
    for h in range(0, 4):
        head_backward(h)
    sp.third(3)
    sp.second(0)
    for h in range(4, 8):
        head_backward(h)
    sp.third(1)
    sp.third(2)
    for h in range(8, H):
        head_backward(h)
    for k in range(3):
        r.rhs1[0:TOK, k * 384 : (k + 1) * 384] = r.qg[:, lanes(k * D + c * 384, 384)]
        one_copies.append(
            push(
                r.qg.at[:, lanes(k * D + (1 - c) * 384, 384)],
                r.rhs1.at[pl.ds(TOK, TOK), pl.ds(k * 384, 384)],
                cp,
            )
        )
    sp.third(0)
    sp.fourth()
    sf.second(3)
    sf.second(1)
    for copy in one_copies + [share_a1, share_at]:
        copy.wait_recv()
    s1.multiply()

    first_grad = jnp.zeros((TOK, D), full)
    for k in range(3):
        first_grad += product_nt(r.qg[:, k * D : (k + 1) * D], w1_cols(k))
    normed = r.normed[...]
    vterm[0:1, :] = jnp.sum(first_grad * normed, axis=0, keepdims=True)
    vterm[1:2, :] = jnp.sum(first_grad, axis=0, keepdims=True)
    vterm[2:3, :] = jnp.sum(r.qg[:, 0:D].astype(full), axis=0, keepdims=True)
    vterm[3:4, :] = jnp.sum(r.qg[:, 2 * D :].astype(full), axis=0, keepdims=True)
    vsend, vrecv = r.vsend, r.vrecv
    vcopy = push(vterm.at[:, lanes((1 - c) * 384, 384)], vrecv.at[0], cp)
    tok_grad = r.resid[...] + norm_back(first_grad, normed, r.inverse[:, 0:1], vector(0))
    tok_out[...] = tok_grad.astype(half)
    sf.third(3)
    vcopy.wait_recv()
    vsend[0] = vterm[:, lanes(c * 384, 384)] + vrecv[0]
    vcopy = push(vsend.at[0], vrecv.at[1], yp)
    sf.second(2)
    sf.third(1)
    sp.fifth()
    for k in range(4):
        block += product(r.hidden[:, k * D : (k + 1) * D], wp_rows(k))
    block_out[...] = block.astype(half)
    sf.second(0)
    sf.third(2)
    vcopy.wait_recv()
    vsend[1] = vsend[0] + vrecv[1]
    vcopy = push(vsend.at[1], vrecv.at[2], xp)
    sf.third(0)
    sf.fourth()
    s1.second(3)
    s1.second(1)
    s1.third(3)
    vcopy.wait_recv()
    vsend[2] = vsend[1] + vrecv[2]
    vcopy = push(vsend.at[2], r.vz.at[0], zp)
    s1.second(2)
    s1.third(1)

    def store_p(owner, value):
        proj_out[:, lanes(owner * 384, 384)] = value

    def store_f(owner, value):
        wide_out[:, lanes(4 * D + owner * F_HALF, F_HALF)] = value

    def store_1(owner, value):
        for k in range(4):
            wide_out[:, lanes(k * D + owner * 384, 384)] = value[:, k * 384 : (k + 1) * 384]

    sp.finish(store_p)
    sf.fifth()
    s1.second(0)
    s1.third(2)
    s1.fourth()
    vcopy.wait_recv()
    r.vz[2] = vsend[2] + r.vz[0]
    vcopy = push(r.vz.at[2], r.vz.at[1], zq)
    s1.third(0)
    vcopy.wait_recv()
    total = r.vz[2] + r.vz[1]
    vsend[3] = total
    vcopy = push(vsend.at[3], vrecv.at[3], cp)
    r.vfull[:, lanes(c * 384, 384)] = total
    sf.finish(store_f)
    s1.fifth()
    vcopy.wait_recv()
    r.vfull[:, lanes((1 - c) * 384, 384)] = vrecv[3]
    shift = D - lax.axis_index("fsdp") * vec.shape[1]
    vec_out[...] = pltpu.roll(r.vfull[...], shift, 1)[0 : vec.shape[0], 0 : vec.shape[1]]
    s1.finish(store_1)
    for copy in sends:
        copy.wait_send()


def block_all(n, tok, lens, cot, wide, proj, vec):
    depth = n // 8
    spaces, parts = scratch_of(depth)
    space = pl.BlockSpec(memory_space=pltpu.VMEM)
    scalars = pl.BlockSpec(memory_space=pltpu.SMEM)
    return pl.pallas_call(
        functools.partial(block_kernel, n, (tuple(spaces), tuple(parts[0]))),
        out_shape=(
            jax.ShapeDtypeStruct((TOK, D), jnp.bfloat16),
            jax.ShapeDtypeStruct((TOK, D), jnp.bfloat16),
            jax.ShapeDtypeStruct((GROUP, 8 * D), jnp.float32),
            jax.ShapeDtypeStruct((P_ROWS, D), jnp.float32),
            jax.ShapeDtypeStruct(vec.shape, jnp.float32),
        ),
        in_specs=[space, scalars, space, space, space, space],
        out_specs=(space,) * 5,
        scratch_shapes=[pltpu.SemaphoreType.DMA((COPIES,))] * 2
        + list(spaces.values())
        + [space for part in parts for space in part.values()],
        compiler_params=pltpu.CompilerParams(
            collective_id=0, has_side_effects=True, vmem_limit_bytes=58 * 2**20
        ),
    )(tok, lens, cot, wide, proj, vec)


def finish_kernel(
    unscale,
    wg,
    pg,
    vg,
    ww,
    pw,
    vw,
    wm,
    pm,
    vm,
    block,
    tok,
    wg_out,
    pg_out,
    vg_out,
    ww_out,
    pw_out,
    vw_out,
    wm_out,
    pm_out,
    vm_out,
    block_out,
    tok_out,
):
    block_out[...] = block[...]
    tok_out[...] = tok[...]
    for grad, old, moment, grad_out, new_out, moment_out, rate, decay in (
        (wg, ww, (wm.at[0], wm.at[1]), wg_out, ww_out, (wm_out.at[0], wm_out.at[1]), rate_matrix, weight_decay),
        (pg, pw, (pm.at[0], pm.at[1]), pg_out, pw_out, (pm_out.at[0], pm_out.at[1]), rate_matrix, weight_decay),
        (vg, vw, (vm.at[:, 0], vm.at[:, 1]), vg_out, vw_out, (vm_out.at[:, 0], vm_out.at[:, 1]), rate_vector, 0.0),
    ):
        gradient = grad[...]
        grad_out[...] = gradient
        scaled_grad = gradient / unscale
        first_moment = beta_one * moment[0][...] + (1.0 - beta_one) * scaled_grad
        second_moment = beta_two * moment[1][...] + (1.0 - beta_two) * scaled_grad * scaled_grad
        corrected_first = first_moment / (1.0 - beta_one**STEP)
        corrected_second = second_moment / (1.0 - beta_two**STEP)
        weights = old[...]
        new_out[...] = weights - rate * (
            corrected_first / (jnp.sqrt(corrected_second) + adam_eps) + decay * weights
        )
        moment_out[0][...] = first_moment
        moment_out[1][...] = second_moment


STEPS = 4


def finish_all(unscale, wg, pg, vg, ww, pw, vw, wm, pm, vm, block, tok):
    vm = vm.transpose(1, 0, 2)
    wide, proj = wg.shape[1] // STEPS, pg.shape[0] // STEPS
    rows, columns = vg.shape
    wide_spec = pl.BlockSpec((GROUP, wide), lambda i: (0, i))
    proj_spec = pl.BlockSpec((proj, D), lambda i: (i, 0))
    vec_spec = pl.BlockSpec((rows, columns), lambda i: (0, 0))
    specs = [wide_spec, proj_spec, vec_spec]
    moments = [
        pl.BlockSpec((2, GROUP, wide), lambda i: (0, 0, i)),
        pl.BlockSpec((2, proj, D), lambda i: (0, i, 0)),
        pl.BlockSpec((rows, 2, columns), lambda i: (0, 0, 0)),
    ]
    flow = [pl.BlockSpec((TOK // STEPS, D), lambda i: (i, 0))] * 2
    arrays = (wg, pg, vg, ww, pw, vw, wm, pm, vm, block, tok)
    shapes = [jax.ShapeDtypeStruct(v.shape, v.dtype) for v in arrays]
    *out, vm, block, tok = pl.pallas_call(
        functools.partial(finish_kernel, unscale),
        grid=(STEPS,),
        out_shape=tuple(shapes),
        in_specs=specs + specs + moments + flow,
        out_specs=tuple(specs + specs + moments + flow),
    )(*arrays)
    return (block, tok, *out, vm.transpose(1, 0, 2))


def body_plain(
    tokens,
    seq_lengths,
    cotangent,
    wide_weights,
    proj_weights,
    vector_params,
    wide_moments,
    proj_moments,
    vector_moments,
):
    shards = (
        wide_weights.astype(jnp.bfloat16),
        proj_weights.astype(jnp.bfloat16),
        vector_params.astype(jnp.bfloat16),
    )
    wide_full, proj_full, vector_full = (
        lax.all_gather(shards[0], "fsdp", axis=0, tiled=True),
        lax.all_gather(shards[1], "fsdp", axis=0, tiled=True),
        lax.all_gather(shards[2], "fsdp", axis=1, tiled=True),
    )
    vectors = vector_full.astype(jnp.float32)
    row_count = tokens.shape[0]
    allowed = allowed_pairs(seq_lengths[0], row_count)
    ratio = FF // D
    local_rows = wide_weights.shape[0]
    unscale = math.sqrt(lax.axis_size("fsdp") * row_count)
    gain_one, shift_one, query_bias, value_bias = (vectors[0], vectors[1], vectors[2], vectors[3])
    out_bias, gain_two, shift_two, proj_bias = (vectors[4], vectors[5], vectors[6], vectors[7])
    fc_bias = vectors[8:].reshape(FF)
    token_float = tokens.astype(jnp.float32)
    first_norm, normed_one, inverse_one = norm_forward(token_float, gain_one, shift_one)
    first_in = first_norm.astype(jnp.bfloat16)
    qkv_bias = jnp.concatenate([query_bias, jnp.zeros_like(query_bias), value_bias])
    qkv_half = (
        jnp.dot(first_in, wide_full[:, : 3 * D], preferred_element_type=jnp.float32) + qkv_bias
    ).astype(jnp.bfloat16)
    queries = qkv_half[:, :D]
    key_rows = qkv_half[:, D : 2 * D]
    value_rows = qkv_half[:, 2 * D :]
    attended, logsum = attention_forward(queries, key_rows, value_rows, allowed)
    residual = (
        token_float
        + jnp.dot(attended, wide_full[:, 3 * D : 4 * D], preferred_element_type=jnp.float32)
        + out_bias
    )
    second_norm, normed_two, inverse_two = norm_forward(residual, gain_two, shift_two)
    second_in = second_norm.astype(jnp.bfloat16)
    before_act = (
        jnp.dot(second_in, wide_full[:, 4 * D :], preferred_element_type=jnp.float32) + fc_bias
    )
    value_part, slope_part = gelu_parts(before_act)
    hidden = value_part.astype(jnp.bfloat16)
    block_output = (
        residual + jnp.dot(hidden, proj_full, preferred_element_type=jnp.float32) + proj_bias
    ).astype(jnp.bfloat16)
    backward_wide, backward_proj, vector_again = wide_full, proj_full, vector_full
    backward_vectors = vector_again.astype(jnp.float32)
    qkv_back = backward_wide[:, : 3 * D]
    out_back = backward_wide[:, 3 * D : 4 * D]
    fc_back = backward_wide[:, 4 * D :]
    cot_float = cotangent.astype(jnp.float32)
    proj_bias_grad = jnp.sum(cot_float, axis=0)
    hidden_grad = jnp.einsum(
        "td,fd->tf", cotangent, backward_proj, preferred_element_type=jnp.float32
    )
    pre_grad = (hidden_grad * slope_part).astype(jnp.bfloat16)
    fc_bias_grad = jnp.sum(pre_grad, axis=0, dtype=jnp.float32)
    second_grad = jnp.einsum("tf,df->td", pre_grad, fc_back, preferred_element_type=jnp.float32)
    resid_norm_grad, gain_two_grad, shift_two_grad = norm_backward(
        second_grad, normed_two, inverse_two, backward_vectors[5]
    )
    resid_grad = cot_float + resid_norm_grad
    mlp_vectors = jnp.concatenate(
        [
            jnp.stack([gain_two_grad, shift_two_grad, proj_bias_grad]),
            fc_bias_grad.reshape(ratio, D),
        ],
        axis=0,
    )
    resid_half = resid_grad.astype(jnp.bfloat16)
    out_bias_grad = jnp.sum(resid_grad, axis=0)
    attended_grad = jnp.einsum(
        "te,de->td", resid_half, out_back, preferred_element_type=jnp.float32
    ).astype(jnp.bfloat16)
    qkv_grad = attention_backward(queries, key_rows, value_rows, allowed, logsum, attended_grad)
    query_bias_grad = jnp.sum(qkv_grad[:, :D], axis=0, dtype=jnp.float32)
    value_bias_grad = jnp.sum(qkv_grad[:, 2 * D :], axis=0, dtype=jnp.float32)
    first_grad = jnp.einsum("tc,dc->td", qkv_grad, qkv_back, preferred_element_type=jnp.float32)
    token_norm_grad, gain_one_grad, shift_one_grad = norm_backward(
        first_grad, normed_one, inverse_one, backward_vectors[0]
    )
    tokens_grad = (resid_grad + token_norm_grad).astype(jnp.bfloat16)
    attn_vectors = jnp.stack(
        [gain_one_grad, shift_one_grad, query_bias_grad, value_bias_grad, out_bias_grad]
    )
    vector_terms = jnp.concatenate([attn_vectors, mlp_vectors], axis=0)
    fc_part = column_term(second_in, pre_grad)
    proj_part = column_term(hidden, cotangent).reshape(
        local_rows * lax.axis_size("fsdp"), ratio * D
    )
    qkv_part = column_term(first_in, qkv_grad)
    out_part = column_term(attended, resid_half)
    joined_shard = lax.psum_scatter(
        jnp.concatenate(
            [
                jnp.concatenate([qkv_part, out_part], axis=1),
                jnp.concatenate([fc_part, proj_part], axis=1),
            ],
            axis=1,
        ),
        "fsdp",
        scatter_dimension=0,
        tiled=True,
    )
    wide_grad = joined_shard[:, : 4 * D + FF]
    proj_grad = joined_shard[:, 4 * D + FF :].reshape(local_rows * ratio, D)
    vector_grad = lax.psum_scatter(vector_terms, "fsdp", scatter_dimension=1, tiled=True)
    wide_new, wide_moments_new = adam_update(
        wide_weights, wide_moments, wide_grad, rate_matrix, weight_decay, unscale
    )
    proj_new, proj_moments_new = adam_update(
        proj_weights, proj_moments, proj_grad, rate_matrix, weight_decay, unscale
    )
    vector_new, vector_moments_new = adam_update(
        vector_params, vector_moments, vector_grad, rate_vector, 0.0, unscale
    )
    return (
        block_output,
        tokens_grad,
        wide_grad,
        proj_grad,
        vector_grad,
        wide_new,
        proj_new,
        vector_new,
        wide_moments_new,
        proj_moments_new,
        vector_moments_new,
    )


def body(
    tokens,
    seq_lengths,
    cotangent,
    wide_weights,
    proj_weights,
    vector_params,
    wide_moments,
    proj_moments,
    vector_moments,
):
    n = lax.axis_size("fsdp")
    if not (n == 32 and wide_weights.shape[0] == GROUP and tokens.shape[0] == TOK):
        return body_plain(
            tokens,
            seq_lengths,
            cotangent,
            wide_weights,
            proj_weights,
            vector_params,
            wide_moments,
            proj_moments,
            vector_moments,
        )
    block_output, tokens_grad, wide_grad, proj_grad, vector_sum = block_all(
        n, tokens, seq_lengths, cotangent, wide_weights, proj_weights, vector_params
    )
    unscale = math.sqrt(n * tokens.shape[0])
    results = finish_all(
        unscale,
        wide_grad,
        proj_grad,
        vector_sum,
        wide_weights,
        proj_weights,
        vector_params,
        wide_moments,
        proj_moments,
        vector_moments,
        block_output,
        tokens_grad,
    )
    return results


def solution(mesh):
    placed = (
        P("fsdp", None),
        P("fsdp", None),
        P("fsdp", None),
        P("fsdp", None),
        P("fsdp", None),
        P(None, "fsdp"),
        P(None, "fsdp", None),
        P(None, "fsdp", None),
        P(None, None, "fsdp"),
    )
    return jax.shard_map(
        body,
        mesh=mesh,
        in_specs=placed,
        out_specs=(
            P("fsdp", None),
            P("fsdp", None),
            P("fsdp", None),
            P("fsdp", None),
            P(None, "fsdp"),
            P("fsdp", None),
            P("fsdp", None),
            P(None, "fsdp"),
            P(None, "fsdp", None),
            P(None, "fsdp", None),
            P(None, None, "fsdp"),
        ),
        check_vma=False,
    )
```
